128 devices in a mesh: ctx: 16 (over x_hi, z, core), ch: 8 (over x_lo, y).
Axes of the slice: x: 4 (x_hi: 2, x_lo: 2; x = x_hi * 2 + x_lo), y: 4, z: 4, core: 2. Of those that a mesh axis runs over, the one named last changes fastest.
Arguments:
- features: bfloat16 [8192, 3, 4096], P('ctx', None, 'ch'), may hold values from -6 to 6
- residual_in: bfloat16 [8192, 4096], P('ctx', 'ch'), may hold values from -6 to 6
- short_filter: float32 [3, 7, 256], P(None, None, 'ch'), may hold values from -2 to 2
- medium_filter: float32 [128, 256], P(None, 'ch'), may hold values from -0.5 to 0.5
- skip_gain: float32 [4096], P('ch'), may hold values from -4 to 4
- out_weight: bfloat16 [4096, 4096], P('ch'), may hold values from -0.125 to 0.125
- norm_gain: float32 [4096], replicated, may hold values from 0.1 to 1.9
- attn_weight: bfloat16 [4096, 12288], P(None, 'ch'), may hold values from -2 to 2, as said below
- attn_out: bfloat16 [4096, 4096], P('ch'), may hold values from -0.125 to 0.125
Outputs:
- result: bfloat16 [8192, 4096], P('ctx', 'ch')
The draws below stay inside these ranges and needn't reach their ends.
Inputs may be any that keep to these rules, and one draw needn't show every extreme that they name: `attn_weight`: entries of order 4096 ** -0.5 times a few.
All inputs are finite; a program needn't handle non-finite values.
Results may differ from the reference program's by a relative error of at most 0.03.
Values may be sent and summed in bfloat16 or wider, within the bound.
A program may use at most 128 MiB of HBM per device.

```python
import jax
import jax.numpy as jnp
from jax import lax

D = 4096
HEAD = 128
GROUP_SIZE = 16
SHORT = 7
MED = 128
HEADS = 32
GROUPS = 256
TOKENS = 8192
N_CH = 8


def draw_attn_weight(key, part):
    first_key = jax.random.fold_in(jax.random.fold_in(key, 17), 0)
    drawn = jnp.clip(jax.random.normal(first_key, (D, HEADS, 3, HEAD), jnp.float32), -5.0, 5.0)
    boosted = jnp.ones((1, HEADS, 1, 1), jnp.float32)
    kind_scale = jnp.array([1.4, 1.4, 4.0], jnp.float32)[None, None, :, None]
    kind_boost = jnp.where(jnp.arange(3)[None, None, :, None] < 2, boosted, 1.0)
    weights = drawn * kind_scale * kind_boost / D ** 0.5
    return weights.reshape(D, HEADS * 3 * HEAD).astype(jnp.bfloat16)


def with_spikes(result, stream_key, source, target, parts, factor):
    def block_of(position):
        return (jnp.arange(result.shape[position]) // (result.shape[position] // parts)).reshape((-1,) + (1,) * (result.ndim - 1 - position))

    one_side = jax.random.permutation(stream_key, parts)[block_of(target)]
    other_side = (block_of(target) + parts // 2) % parts
    return jnp.where((block_of(source) == one_side) | (block_of(source) == other_side), factor * result, result)


def shard_levels(rng, extent, cuts, smallest, top_value):
    gain = 1.0
    for dim, parts in cuts:
        draws = jax.random.uniform(jax.random.fold_in(jax.random.fold_in(rng, 6), dim), (parts,), jnp.float32, smallest / len(cuts), top_value / len(cuts))
        gain = gain * jnp.repeat(jnp.exp(draws), extent[dim] // parts).reshape((-1,) + (1,) * (len(extent) - 1 - dim))
    return gain


def gaussian(stream_key, shape, scale, bound, shards=(), held_as=jnp.bfloat16):
    entries = jax.random.normal(stream_key, shape, jnp.float32) * scale
    if len(shards) > 0:
        entries = shard_levels(stream_key, shape, shards, -0.22, 0.18) * entries
    return jnp.clip(entries, min=-bound, max=bound).astype(held_as)


def heavy_noise(own_key, shape, width, limit, shards, heavy, kind=jnp.bfloat16):
    values = width * jax.random.normal(own_key, shape, jnp.float32)
    if shards:
        values = values * shard_levels(own_key, shape, shards, -0.22, 0.18)
    return jnp.clip(with_spikes(values, jax.random.fold_in(own_key, 3), *heavy), -limit, limit).astype(kind)


def setup_inputs(seed: int = 0) -> dict:
    keys = jax.random.split(jax.random.key(seed), 10)
    return {
        "features": gaussian(keys[0], (TOKENS, 3, D), 1.0, 6.0, ((0, 16), (2, 8))),
        "residual_in": gaussian(keys[1], (TOKENS, D), 1.0, 6.0, ((0, 16), (1, 8))),
        "short_filter": gaussian(keys[2], (3, SHORT, GROUPS), SHORT ** -0.5, 2.0, ((2, 8),), jnp.float32),
        "medium_filter": gaussian(keys[3], (MED, GROUPS), MED ** -0.5, 0.5, ((1, 8),), jnp.float32),
        "skip_gain": gaussian(keys[4], (D,), 1.0, 4.0, ((0, 8),), jnp.float32),
        "out_weight": heavy_noise(keys[5], (D, D), D ** -0.5, 0.125, ((0, 8),), (0, 1, 8, 2.0)),
        "norm_gain": jnp.clip(1.0 + 0.18 * jax.random.normal(keys[6], (D,), jnp.float32), 0.1, 1.9),
        "attn_weight": draw_attn_weight(jax.random.fold_in(keys[9], 71), 0),
        "attn_out": heavy_noise(keys[8], (HEADS * HEAD, D), (HEADS * HEAD) ** -0.5, 0.125, ((0, 8),), (0, 1, 8, 2.0)),
    }


def rotate_rows(block, positions):
    half_size = block.shape[-1] // 2
    frequency = 10000.0 ** (-jnp.arange(half_size, dtype=jnp.float32) * 2.0 / block.shape[-1])
    angles = positions.astype(jnp.float32)[:, None] * frequency[None, :]
    cosine = jnp.cos(angles)[:, None, :]
    sine_part = jnp.sin(angles)[:, None, :]
    first_half = block[..., :half_size]
    second_half = block[..., half_size:]
    return jnp.concatenate([first_half * cosine - second_half * sine_part, second_half * cosine + first_half * sine_part], axis=-1)

def blockwise_sum(left, right, block_count):
    width_block = left.shape[1] // block_count
    summed = jnp.zeros((left.shape[0], right.shape[1]), jnp.float32)
    for block_index in range(block_count):
        lower = block_index * width_block
        partial_term = jnp.dot(left[:, lower:lower + width_block], right[lower:lower + width_block], preferred_element_type=jnp.float32).astype(jnp.bfloat16)
        summed = summed + lax.optimization_barrier(partial_term).astype(jnp.float32)
    return summed

def reference(features, residual_in, short_filter, medium_filter, skip_gain, out_weight, norm_gain, attn_weight, attn_out):
    widened = features.astype(jnp.float32)
    short_taps = jnp.repeat(short_filter, GROUP_SIZE, axis=2)
    padded = jnp.pad(widened, ((SHORT - 1, 0), (0, 0), (0, 0)))
    featured = jnp.zeros(widened.shape, jnp.float32)
    for tap_index in range(SHORT):
        begin_row = SHORT - 1 - tap_index
        featured = featured + short_taps[:, tap_index, :][None] * padded[begin_row:begin_row + TOKENS]
    product = (featured[:, 1, :] * featured[:, 2, :]).astype(jnp.bfloat16)
    medium_taps = jnp.repeat(medium_filter, GROUP_SIZE, axis=1)
    product_pad = jnp.pad(product.astype(jnp.float32), ((MED - 1, 0), (0, 0)))

    def add_tap(tap_index, accum):
        begin_row = (MED - 1 - tap_index).astype(jnp.int32)
        window = lax.dynamic_slice_in_dim(product_pad, begin_row, TOKENS, 0)
        tap_row = lax.dynamic_index_in_dim(medium_taps, tap_index.astype(jnp.int32), 0, keepdims=False)
        return accum + tap_row[None, :] * window
    mixed = lax.fori_loop(0, MED, add_tap, jnp.zeros((TOKENS, D), jnp.float32))
    mixed = mixed + skip_gain[None, :] * product.astype(jnp.float32)
    gated = (featured[:, 0, :] * mixed).astype(jnp.bfloat16)
    hyena_out = blockwise_sum(gated, out_weight, N_CH)
    stream = (residual_in.astype(jnp.float32) + hyena_out).astype(jnp.bfloat16)
    stream_wide = stream.astype(jnp.float32)
    inverse = lax.rsqrt(lax.optimization_barrier(jnp.mean(stream_wide * stream_wide, axis=1)) + 1e-05)
    normed = (stream_wide * inverse[:, None] * norm_gain[None, :]).astype(jnp.bfloat16)
    projected = jnp.dot(normed, attn_weight, preferred_element_type=jnp.float32).reshape(TOKENS, HEADS, 3, HEAD)
    positions = jnp.arange(TOKENS, dtype=jnp.int32)
    queries = rotate_rows(projected[:, :, 0, :], positions).astype(jnp.bfloat16)
    key_rows = rotate_rows(projected[:, :, 1, :], positions).astype(jnp.bfloat16)
    value_rows = projected[:, :, 2, :].astype(jnp.bfloat16)
    causal = positions[None, :] <= positions[:, None]
    scale_factor = 1.0 / HEAD ** 0.5

    def one_head(operands):
        query_head, key_head, value_head = operands
        scores = jnp.dot(query_head, key_head.T, preferred_element_type=jnp.float32) * scale_factor
        scores = jnp.where(causal, scores, -1e+30)
        row_max = lax.optimization_barrier(jnp.max(scores, axis=1, keepdims=True))
        weights = jnp.where(causal, jnp.exp(scores - row_max), 0.0)
        row_total = lax.optimization_barrier(jnp.sum(weights, axis=1, keepdims=True))
        output = jnp.dot(weights.astype(jnp.bfloat16), value_head, preferred_element_type=jnp.float32) / row_total
        return output.astype(jnp.bfloat16)
    attended = lax.map(one_head, (jnp.transpose(queries, (1, 0, 2)), jnp.transpose(key_rows, (1, 0, 2)), jnp.transpose(value_rows, (1, 0, 2))))
    attended = jnp.transpose(attended, (1, 0, 2)).reshape(TOKENS, HEADS * HEAD)
    attn_mix = blockwise_sum(attended, attn_out, N_CH)
    return (stream_wide + attn_mix).astype(jnp.bfloat16)
```

```python
import functools

import jax
import jax.numpy as jnp
from jax import lax
from jax.experimental import pallas as pl
from jax.experimental.pallas import tpu as pltpu
from jax.sharding import PartitionSpec as P

HEAD = 128
GROUP_SIZE = 16
N_CH = 8
N_CTX = 16
N_Y = 4
N_Z = 4
HALO = 144

norm_eps = 1e-05
MESH = pl.DeviceIdType.MESH
VMEM_LIMIT = 60 * 1024 * 1024


def remote(src, dst, send_sem, recv_sem, target):
    return pltpu.make_async_remote_copy(
        src_ref=src, dst_ref=dst, send_sem=send_sem, recv_sem=recv_sem,
        device_id=target, device_id_type=MESH,
    )


def greet(targets):
    barrier = pltpu.get_barrier_semaphore()
    for target in targets:
        pl.semaphore_signal(barrier, inc=1, device_id=target, device_id_type=MESH)
    pl.semaphore_wait(barrier, len(targets))


def whole(count):
    return [pl.BlockSpec(memory_space=pltpu.VMEM)] * count


def hyena_kernel(feat_ref, short_ref, medium_ref, skip_ref, out_ref,
                 halo, ext, taps, product, product_t, query, mixed_t, send_sem, recv_sem):
    rows, chans = out_ref.shape
    ctx = lax.axis_index("ctx")
    chan = lax.axis_index("ch")
    after = (lax.rem(ctx + 1, N_CTX), chan)
    before = (lax.rem(ctx + N_CTX - 1, N_CTX), chan)
    greet([after, before])
    near = remote(feat_ref.at[pl.ds(0, 1), pl.ds(rows - 16, 16)], halo.at[pl.ds(0, 1), pl.ds(HALO - 16, 16)],
                  send_sem.at[0], recv_sem.at[0], after)
    far = remote(feat_ref.at[pl.ds(1, 2), pl.ds(rows - HALO, HALO)], halo.at[pl.ds(1, 2)],
                 send_sem.at[1], recv_sem.at[1], after)
    near.start()
    far.start()

    groups = short_ref.shape[2]
    spread = (lax.broadcasted_iota(jnp.int32, (groups, chans), 1) // GROUP_SIZE
              == lax.broadcasted_iota(jnp.int32, (groups, chans), 0)).astype(jnp.float32)
    for kind in range(3):
        taps[kind, 0:7, :] = jnp.dot(short_ref[kind], spread, preferred_element_type=jnp.float32,
                                     precision=lax.Precision.HIGHEST)
        ext[kind, HALO:, :] = feat_ref[kind].astype(jnp.float32)

    def featured(kind, first, count):
        slab = ext[kind, pl.ds(first - 8 if isinstance(first, int) else pl.multiple_of(first - 8, 8), count + 8), :]
        total = taps[kind, 0:1, :] * slab[8:]
        for tap in range(1, 7):
            total = total + taps[kind, tap : tap + 1, :] * pltpu.roll(slab, tap, 0)[8:]
        return total

    def main_rows(step, carry):
        first = pl.multiple_of(16 + step * 16, 16)
        query[pl.ds(first, 16), :] = featured(0, pl.multiple_of(first + HALO, 16), 16)
        product[pl.ds(first + 128, 16), :] = featured(1, pl.multiple_of(first + HALO, 16), 16) * featured(2, pl.multiple_of(first + HALO, 16), 16)
        return carry

    lax.fori_loop(0, rows // 16 - 1, main_rows, 0)
    near.wait()
    far.wait()
    keep = (ctx > 0).astype(jnp.float32)
    ext[0, HALO - 16 : HALO, :] = halo[0, HALO - 16 : HALO, :].astype(jnp.float32) * keep
    for kind in (1, 2):
        ext[kind, 0:HALO, :] = halo[kind].astype(jnp.float32) * keep
    query[0:16, :] = featured(0, HALO, 16)

    def rim_rows(step, carry):
        first = pl.multiple_of(step * 16, 16)
        product[pl.ds(first, 16), :] = featured(1, pl.multiple_of(first + 16, 16), 16) * featured(2, pl.multiple_of(first + 16, 16), 16)
        return carry

    lax.fori_loop(0, 9, rim_rows, 0)
    for block in range(5):
        product_t[:, 128 * block : 128 * block + 128] = (
            product[128 * block : 128 * block + 128, :].T.astype(jnp.bfloat16))
    row = lax.broadcasted_iota(jnp.int32, (128, 128), 0)
    col = lax.broadcasted_iota(jnp.int32, (128, 128), 1)

    def one_group(group, carry):
        line = jnp.broadcast_to(medium_ref[pl.ds(group, 1), :], (128, 128))
        wheel = pltpu.roll(line, 0, 1, stride=1, stride_axis=0)
        table = jnp.concatenate([jnp.where(col < row, wheel, 0.0), jnp.where(col >= row, wheel, 0.0)],
                                axis=0).astype(jnp.bfloat16)
        lane = pl.ds(pl.multiple_of(group * GROUP_SIZE, GROUP_SIZE), GROUP_SIZE)
        window = jnp.concatenate(
            [product_t[lane, 128 * block : 128 * block + 256] for block in range(4)], axis=0)
        mix = jnp.dot(window, table, preferred_element_type=jnp.float32)
        for block in range(4):
            mixed_t[lane, 128 * block : 128 * block + 128] = mix[16 * block : 16 * block + 16, :]
        return carry

    lax.fori_loop(0, groups, one_group, 0)
    for block in range(4):
        part = pl.ds(128 * block, 128)
        mix = mixed_t[:, part].T
        inner = product[pl.ds(128 * block + 128, 128), :].astype(jnp.bfloat16).astype(jnp.float32)
        out_ref[part, :] = (query[part, :] * (mix + skip_ref[...] * inner)).astype(jnp.bfloat16)


def hyena(feats, short_filter, medium_t, skip_row):
    kinds, rows, chans = feats.shape
    return pl.pallas_call(
        hyena_kernel,
        out_shape=jax.ShapeDtypeStruct((rows, chans), jnp.bfloat16),
        in_specs=whole(4),
        out_specs=pl.BlockSpec(memory_space=pltpu.VMEM),
        scratch_shapes=[
            pltpu.VMEM((3, HALO, chans), jnp.bfloat16),
            pltpu.VMEM((3, HALO + rows, chans), jnp.float32),
            pltpu.VMEM((3, 8, chans), jnp.float32),
            pltpu.VMEM((128 + rows, chans), jnp.float32),
            pltpu.VMEM((chans, 128 + rows), jnp.bfloat16),
            pltpu.VMEM((rows, chans), jnp.float32),
            pltpu.VMEM((chans, rows), jnp.float32),
            pltpu.SemaphoreType.DMA((2,)),
            pltpu.SemaphoreType.DMA((2,)),
        ],
        compiler_params=pltpu.CompilerParams(collective_id=0, has_side_effects=True, vmem_limit_bytes=VMEM_LIMIT),
        name="hyena",
    )(feats, short_filter, medium_t, skip_row)


def project_kernel(left_ref, base_ref, own_ref, other_ref, out_ref,
                   w_own, w_other, left_in, outbox, inbox, kept,
                   w_sem, x_send, x_recv, y_send, y_recv):
    rows, depth = left_ref.shape
    width = depth
    ctx = lax.axis_index("ctx")
    chan = lax.axis_index("ch")
    y_pos = lax.rem(chan, N_Y)
    x_lo = chan // N_Y
    partner = (ctx, (1 - x_lo) * N_Y + y_pos)
    column = [(ctx, x_lo * N_Y + lax.rem(y_pos + step, N_Y)) for step in range(1, N_Y)]
    half = pl.ds(pl.multiple_of(x_lo * (N_Y * width), N_Y * width), N_Y * width)
    load_own = pltpu.make_async_copy(own_ref.at[:, half], w_own, w_sem.at[0])
    load_other = pltpu.make_async_copy(other_ref, w_other, w_sem.at[1])
    load_own.start()
    load_other.start()
    greet([partner] + column)
    pieces = 4
    tall = rows // pieces
    crossing = []
    for piece in range(pieces):
        part = pl.ds(piece * tall, tall)
        copy = remote(left_ref.at[part], left_in.at[part], x_send.at[piece], x_recv.at[piece], partner)
        copy.start()
        crossing.append(copy)
    load_own.wait()
    load_other.wait()
    sent = []
    for piece in range(pieces):
        part = pl.ds(piece * tall, tall)
        crossing[piece].wait_recv()
        mine = left_ref[part, :]
        theirs = left_in[part, :]
        for step in (2, 1, 3, 0):
            target = lax.rem(y_pos + step, N_Y)
            cols = pl.ds(pl.multiple_of(target * width, width), width)
            term = (jnp.dot(mine, w_own[:, cols], preferred_element_type=jnp.float32)
                    + jnp.dot(theirs, w_other[:, cols], preferred_element_type=jnp.float32))
            if step == 0:
                kept[part, :] = term + base_ref[part, :].astype(jnp.float32)
            else:
                outbox[step - 1, part, :] = term.astype(jnp.bfloat16)
                copy = remote(outbox.at[step - 1, part], inbox.at[step - 1, part],
                              y_send.at[step - 1, piece], y_recv.at[step - 1, piece], column[step - 1])
                copy.start()
                sent.append(copy)
    for piece in range(pieces):
        part = pl.ds(piece * tall, tall)
        total = kept[part, :]
        for step in (2, 1, 3):
            sent[piece * 3 + (2, 1, 3).index(step)].wait_recv()
            total = total + inbox[step - 1, part, :].astype(jnp.float32)
        out_ref[part, :] = total.astype(jnp.bfloat16)
    for copy in crossing + sent:
        copy.wait_send()


def project(left, base, own_weight, other_half, collective_id):
    rows, depth = left.shape
    width = depth
    return pl.pallas_call(
        project_kernel,
        out_shape=jax.ShapeDtypeStruct((rows, width), jnp.bfloat16),
        in_specs=whole(2) + [pl.BlockSpec(memory_space=pl.ANY)] * 2,
        out_specs=pl.BlockSpec(memory_space=pltpu.VMEM),
        scratch_shapes=[
            pltpu.VMEM((depth, N_Y * width), jnp.bfloat16),
            pltpu.VMEM((depth, N_Y * width), jnp.bfloat16),
            pltpu.VMEM((rows, depth), jnp.bfloat16),
            pltpu.VMEM((3, rows, width), jnp.bfloat16),
            pltpu.VMEM((3, rows, width), jnp.bfloat16),
            pltpu.VMEM((rows, width), jnp.float32),
            pltpu.SemaphoreType.DMA((2,)),
            pltpu.SemaphoreType.DMA((4,)),
            pltpu.SemaphoreType.DMA((4,)),
            pltpu.SemaphoreType.DMA((3, 4)),
            pltpu.SemaphoreType.DMA((3, 4)),
        ],
        compiler_params=pltpu.CompilerParams(collective_id=collective_id, has_side_effects=True,
                                             vmem_limit_bytes=VMEM_LIMIT),
        name="project",
    )(left, base, own_weight, other_half)


def partner_half(weight):
    rows, cols = weight.shape
    chan = lax.axis_index("ch")
    ctx = lax.axis_index("ctx")
    x_lo = chan // N_Y
    piece = lax.dynamic_slice(weight, (ctx * (rows // N_CTX), (1 - x_lo) * (cols // 2)), (rows // N_CTX, cols // 2))
    piece = lax.ppermute(piece, "ch", [(source, (source + N_Y) % N_CH) for source in range(N_CH)])
    return lax.all_gather(piece, "ctx", axis=0, tiled=True)


def qkv_kernel(stream_ref, gain_ref, cos_ref, sin_ref, w_hbm, out_ref,
               blocks, w_ref, acc, squares, w_sem, send_sem, recv_sem):
    rows, width = stream_ref.shape
    ctx = lax.axis_index("ctx")
    chan = lax.axis_index("ch")
    y_pos = lax.rem(chan, N_Y)
    x_lo = chan // N_Y
    x_hi = 1 - x_lo
    up, down, opposite = lax.rem(y_pos + 1, N_Y), lax.rem(y_pos + 3, N_Y), lax.rem(y_pos + 2, N_Y)
    dev_up = (ctx, x_lo * N_Y + up)
    dev_down = (ctx, x_lo * N_Y + down)
    dev_x = (ctx, x_hi * N_Y + y_pos)
    load = pltpu.make_async_copy(w_hbm, w_ref, w_sem)
    load.start()
    greet([dev_up, dev_down, dev_x])
    tall = rows // 2
    halves = [pl.ds(0, tall), pl.ds(tall, tall)]

    def slot(x, y):
        return x * N_Y + y

    sent = {}

    def push(name, src, where, part, target):
        index = len(sent)
        copy = remote(src, blocks.at[where, part], send_sem.at[index], recv_sem.at[index], target)
        copy.start()
        sent[name] = copy

    mine = slot(x_lo, y_pos)
    for number, part in enumerate(halves):
        push(("x", number), stream_ref.at[part], mine, part, dev_x)
        push(("up", number), stream_ref.at[part], mine, part, dev_up)
        push(("down", number), stream_ref.at[part], mine, part, dev_down)

    load.wait()
    squares[...] = jnp.zeros_like(squares)

    def use(block, where, first):
        wide = block.astype(jnp.float32)
        square = wide * wide
        squares[...] += (square[:, 0:128] + square[:, 128:256]) + (square[:, 256:384] + square[:, 384:512])
        cols = pl.ds(pl.multiple_of(where * width, width), width)
        scaled = (wide * gain_ref[:, cols]).astype(jnp.bfloat16)
        term = jnp.dot(scaled, w_ref[cols, :], preferred_element_type=jnp.float32)
        acc[...] = term if first else acc[...] + term

    use(stream_ref[...], mine, True)
    sent["up", 0].wait_recv()
    push(("upup", 0), blocks.at[slot(x_lo, down), halves[0]], slot(x_lo, down), halves[0], dev_up)
    sent["down", 0].wait_recv()
    sent["down", 1].wait_recv()
    push(("downdown", 0), blocks.at[slot(x_lo, up), halves[1]], slot(x_lo, up), halves[1], dev_down)
    sent["x", 0].wait_recv()
    other = slot(x_hi, y_pos)
    push(("xup", 0), blocks.at[other, halves[0]], other, halves[0], dev_up)
    push(("xdown", 0), blocks.at[other, halves[0]], other, halves[0], dev_down)
    sent["x", 1].wait_recv()
    push(("xup", 1), blocks.at[other, halves[1]], other, halves[1], dev_up)
    push(("xdown", 1), blocks.at[other, halves[1]], other, halves[1], dev_down)
    use(blocks[slot(x_lo, up)], slot(x_lo, up), False)
    sent["upup", 0].wait_recv()
    far = slot(x_lo, opposite)
    push(("far", 0), blocks.at[far, halves[0]], far, halves[0], dev_x)
    sent["downdown", 0].wait_recv()
    push(("far", 1), blocks.at[far, halves[1]], far, halves[1], dev_x)
    sent["up", 1].wait_recv()
    use(blocks[slot(x_lo, down)], slot(x_lo, down), False)
    use(blocks[other], other, False)
    use(blocks[far], far, False)
    for name, y in (("xdown", up), ("xup", down), ("far", opposite)):
        sent[name, 0].wait_recv()
        sent[name, 1].wait_recv()
        use(blocks[slot(x_hi, y)], slot(x_hi, y), False)

    inverse = lax.rsqrt(jnp.sum(squares[...], axis=1, keepdims=True) / (N_CH * width) + norm_eps)
    scale = HEAD ** -0.5 * 1.4426950408889634
    for head in range(4):
        for kind in range(3):
            first = (head * 3 + kind) * HEAD
            value = acc[:, first : first + HEAD] * inverse
            if kind < 2:
                value = value * cos_ref[...] + pltpu.roll(value, HEAD // 2, 1) * sin_ref[...]
            if kind == 0:
                value = value * scale
            out_ref[head, kind] = value.astype(jnp.bfloat16)
    for copy in sent.values():
        copy.wait_send()


def gathered_qkv(stream, gain_row, cosine, sine, weight):
    rows, width = stream.shape
    heads = weight.shape[1] // (3 * HEAD)
    return pl.pallas_call(
        qkv_kernel,
        out_shape=jax.ShapeDtypeStruct((heads, 3, rows, HEAD), jnp.bfloat16),
        in_specs=whole(4) + [pl.BlockSpec(memory_space=pl.ANY)],
        out_specs=pl.BlockSpec(memory_space=pltpu.VMEM),
        scratch_shapes=[
            pltpu.VMEM((N_CH, rows, width), jnp.bfloat16),
            pltpu.VMEM(weight.shape, jnp.bfloat16),
            pltpu.VMEM((rows, weight.shape[1]), jnp.float32),
            pltpu.VMEM((rows, 128), jnp.float32),
            pltpu.SemaphoreType.DMA,
            pltpu.SemaphoreType.DMA((14,)),
            pltpu.SemaphoreType.DMA((14,)),
        ],
        compiler_params=pltpu.CompilerParams(collective_id=2, has_side_effects=True, vmem_limit_bytes=VMEM_LIMIT),
        name="gather_qkv",
    )(stream, gain_row, cosine, sine, weight)


def attention_kernel(qkv_ref, out_ref, queries, keyvals, acc, peak, outbox,
                     own_sem, q_send, q_recv, z_send, z_recv, s_send, s_recv,
                     h_send, h_recv, t_send, t_recv, o_send, o_recv):
    heads, kinds, rows, head = qkv_ref.shape
    ctx = lax.axis_index("ctx")
    chan = lax.axis_index("ch")
    core = lax.rem(ctx, 2)
    z_pos = lax.rem(ctx // 2, N_Z)
    high = ctx // (2 * N_Z)

    def place(x, z, c):
        return ((x * N_Z + z) * 2 + c, chan)

    sibling = place(high, z_pos, 1 - core)
    across = place(1 - high, z_pos, core)
    ring = [place(high, lax.rem(z_pos + step, N_Z), core) for step in range(1, N_Z)]
    greet(ring + [sibling, across])

    def source(step):
        return lax.rem(z_pos + N_Z - step, N_Z)

    own_q = pltpu.make_async_copy(qkv_ref.at[z_pos, 0], queries.at[z_pos], own_sem.at[0])
    own_kv = pltpu.make_async_copy(qkv_ref.at[z_pos, pl.ds(1, 2)], keyvals.at[high, z_pos, core], own_sem.at[1])
    own_kv.start()
    own_q.start()
    z_copies, q_copies = [], []
    for step in (1, 2, 3):
        target = lax.rem(z_pos + step, N_Z)
        copy = remote(qkv_ref.at[target, pl.ds(1, 2)], keyvals.at[high, z_pos, core],
                      z_send.at[step - 1], z_recv.at[step - 1], ring[step - 1])
        copy.start()
        z_copies.append(copy)
    for step in (1, 2, 3):
        target = lax.rem(z_pos + step, N_Z)
        copy = remote(qkv_ref.at[target, 0], queries.at[z_pos],
                      q_send.at[step - 1], q_recv.at[step - 1], ring[step - 1])
        copy.start()
        q_copies.append(copy)
    shares, hops = [], []

    def spread(step):
        place_here = keyvals.at[high, source(step), core]
        share = remote(place_here, place_here, s_send.at[step], s_recv.at[step], sibling)
        share.start()
        shares.append(share)
        hop = remote(place_here, place_here, h_send.at[step], h_recv.at[step], across)
        hops.append(hop)

        @pl.when(high == 0)
        def _():
            hop.start()

    own_kv.wait()
    spread(0)
    for step in (1, 3, 2):
        z_copies[step - 1].wait_recv()
        spread(step)
    own_q.wait()
    for copy in q_copies:
        copy.wait_recv()
    for share in shares:
        share.wait_recv()

    row = lax.broadcasted_iota(jnp.int32, (rows, rows), 0)
    col = lax.broadcasted_iota(jnp.int32, (rows, rows), 1)
    ones = jnp.ones((rows, head), jnp.bfloat16)

    def update(block, x, z, c, diagonal):
        scores = lax.dot_general(queries[block], keyvals[x, z, c, 0], (((1,), (1,)), ((), ())),
                                 preferred_element_type=jnp.float32)
        if diagonal:
            scores = jnp.where(col <= row, scores, -1e30)
        top = jnp.max(scores, axis=1, keepdims=True)
        if not diagonal:
            old = peak[block]
            new = jnp.maximum(old, top)
            peak[block] = new
            shrink = jnp.exp2(old - new)[:, 0:1]
        else:
            new = jnp.broadcast_to(top, (rows, head))
            peak[block] = new
        weights = jnp.exp2(scores - new[:, 0:1]).astype(jnp.bfloat16)
        wide = jnp.concatenate([keyvals[x, z, c, 1], ones], axis=1)
        term = jnp.dot(weights, wide, preferred_element_type=jnp.float32)
        acc[block] = term if diagonal else acc[block] * shrink + term

    def own_part(block, carry):
        update(block, high, block, core, True)

        def earlier(index, inner):
            update(block, high, index // 2, lax.rem(index, 2), False)
            return inner

        lax.fori_loop(0, 2 * block + core, earlier, 0)
        return carry

    lax.fori_loop(0, N_Z, own_part, 0)

    @pl.when(high == 1)
    def _():
        passes = []
        for order, step in enumerate((0, 1, 3, 2)):
            hops[order].wait_recv()
            landed = keyvals.at[0, source(step), core]
            copy = remote(landed, landed, t_send.at[step], t_recv.at[step], sibling)
            copy.start()
            passes.append(copy)
        for copy in passes:
            copy.wait_recv()

        def low_part(block, carry):
            def each(index, inner):
                update(block, 0, index // 2, lax.rem(index, 2), False)
                return inner

            lax.fori_loop(0, 2 * N_Z, each, 0)
            return carry

        lax.fori_loop(0, N_Z, low_part, 0)
        for copy in passes:
            copy.wait_send()

    backs = []
    for step in (2, 1, 3, 0):
        target = lax.rem(z_pos + step, N_Z)
        result = acc[target]
        outbox[target] = (result[:, :head] / result[:, head:]).astype(jnp.bfloat16)
        lanes = pl.ds(pl.multiple_of(z_pos * head, head), head)
        if step == 0:
            out_ref[:, lanes] = outbox[target]
        else:
            copy = remote(outbox.at[target], out_ref.at[:, lanes], o_send.at[step - 1], o_recv.at[step - 1],
                          ring[step - 1])
            copy.start()
            backs.append(copy)
    for copy in backs:
        copy.wait_recv()
    for copy in z_copies + q_copies + shares + backs:
        copy.wait_send()

    @pl.when(high == 0)
    def _():
        for hop in hops:
            hop.wait_send()


def attention(qkv):
    heads, kinds, rows, head = qkv.shape
    dma = pltpu.SemaphoreType.DMA
    return pl.pallas_call(
        attention_kernel,
        out_shape=jax.ShapeDtypeStruct((rows, heads * head), jnp.bfloat16),
        in_specs=whole(1),
        out_specs=pl.BlockSpec(memory_space=pltpu.VMEM),
        scratch_shapes=[
            pltpu.VMEM((N_Z, rows, head), jnp.bfloat16),
            pltpu.VMEM((2, N_Z, 2, 2, rows, head), jnp.bfloat16),
            pltpu.VMEM((N_Z, rows, 2 * head), jnp.float32),
            pltpu.VMEM((N_Z, rows, head), jnp.float32),
            pltpu.VMEM((N_Z, rows, head), jnp.bfloat16),
            dma((2,)), dma((3,)), dma((3,)), dma((3,)), dma((3,)), dma((4,)), dma((4,)),
            dma((4,)), dma((4,)), dma((4,)), dma((4,)), dma((3,)), dma((3,)),
        ],
        compiler_params=pltpu.CompilerParams(collective_id=3, has_side_effects=True, vmem_limit_bytes=VMEM_LIMIT),
        name="attention",
    )(qkv)


def rotation_tables(rows):
    positions = lax.axis_index("ctx") * rows + jnp.arange(rows, dtype=jnp.int32)
    half_size = HEAD // 2
    frequency = 10000.0 ** (-jnp.arange(half_size, dtype=jnp.float32) * 2.0 / HEAD)
    angles = positions.astype(jnp.float32)[:, None] * frequency[None, :]
    cosine, sine = jnp.cos(angles), jnp.sin(angles)
    return jnp.concatenate([cosine, cosine], axis=1), jnp.concatenate([-sine, sine], axis=1)


def shards(features, residual_in, short_filter, medium_filter, skip_gain, out_weight, norm_gain, attn_weight,
           attn_out):
    rows = features.shape[0]
    out_half = partner_half(out_weight)
    attn_half = partner_half(attn_out)
    cosine, sine = rotation_tables(rows)
    gated = hyena(jnp.transpose(features, (1, 0, 2)), short_filter, medium_filter.T, skip_gain[None, :])
    stream = project(gated, residual_in, out_weight, out_half, 1)
    qkv = gathered_qkv(stream, norm_gain[None, :], cosine, sine, attn_weight)
    attended = attention(qkv)
    return project(attended, stream, attn_out, attn_half, 4)


def solution(mesh):
    in_specs = (
        P("ctx", None, "ch"),
        P("ctx", "ch"),
        P(None, None, "ch"),
        P(None, "ch"),
        P("ch"),
        P("ch", None),
        P(),
        P(None, "ch"),
        P("ch", None),
    )
    out_specs = P("ctx", "ch")
    return jax.shard_map(shards, mesh=mesh, in_specs=in_specs, out_specs=out_specs, check_vma=False)
```

```python
import functools

import jax
import jax.numpy as jnp
from jax import lax
from jax.experimental import pallas as pl
from jax.experimental.pallas import tpu as pltpu
from jax.sharding import PartitionSpec as P

HEAD = 128
GROUP_SIZE = 16
N_CH = 8
N_CTX = 16
N_Y = 4
N_Z = 4
HALO = 144

norm_eps = 1e-05
MESH = pl.DeviceIdType.MESH
VMEM_LIMIT = 60 * 1024 * 1024


def remote(src, dst, send_sem, recv_sem, target):
    return pltpu.make_async_remote_copy(
        src_ref=src, dst_ref=dst, send_sem=send_sem, recv_sem=recv_sem,
        device_id=target, device_id_type=MESH,
    )


def greet(targets):
    barrier = pltpu.get_barrier_semaphore()
    for target in targets:
        pl.semaphore_signal(barrier, inc=1, device_id=target, device_id_type=MESH)
    pl.semaphore_wait(barrier, len(targets))


def whole(count):
    return [pl.BlockSpec(memory_space=pltpu.VMEM)] * count


def ring_z():
    ctx = lax.axis_index("ctx")
    chan = lax.axis_index("ch")
    core = lax.rem(ctx, 2)
    z_pos = lax.rem(ctx // 2, N_Z)
    base = ctx - z_pos * 2 - core
    sibling = (base + z_pos * 2 + 1 - core, chan)
    ring = [(base + lax.rem(z_pos + step, N_Z) * 2 + core, chan) for step in range(1, N_Z)]
    return core, z_pos, sibling, ring


def piece_rows(z_pos, core, tall):
    return pl.ds(pl.multiple_of((z_pos * 2 + core) * tall, tall), tall)


class Spread:
    def __init__(self, piece_ref, whole_ref, send_sem, recv_sem):
        self.piece, self.whole = piece_ref, whole_ref
        self.send, self.recv = send_sem, recv_sem
        self.core, self.z_pos, self.sibling, self.ring = ring_z()
        self.tall = whole_ref.shape[0] // (2 * N_Z)
        self.copies = []

    def push(self, src, rows, target):
        index = len(self.copies)
        copy = remote(src, self.whole.at[rows], self.send.at[index], self.recv.at[index], target)
        copy.start()
        self.copies.append(copy)

    def first(self):
        rows = piece_rows(self.z_pos, self.core, self.tall)
        for target in self.ring + [self.sibling]:
            self.push(self.piece, rows, target)

    def second(self):
        for step in (1, 3, 2):
            self.copies[step - 1].wait_recv()
            rows = piece_rows(lax.rem(self.z_pos + N_Z - step, N_Z), self.core, self.tall)
            self.push(self.whole.at[rows], rows, self.sibling)

    def finish(self):
        for copy in self.copies[3:]:
            copy.wait_recv()
        for copy in self.copies:
            copy.wait_send()


PIECES = 4


def column_places():
    ctx = lax.axis_index("ctx")
    chan = lax.axis_index("ch")
    y_pos = lax.rem(chan, N_Y)
    x_lo = chan // N_Y
    partner = (ctx, (1 - x_lo) * N_Y + y_pos)
    up = (ctx, x_lo * N_Y + lax.rem(y_pos + 1, N_Y))
    down = (ctx, x_lo * N_Y + lax.rem(y_pos + 3, N_Y))
    return y_pos, x_lo, partner, up, down


def piece_of(ref, piece):
    tall = ref.shape[0] // PIECES
    return ref.at[pl.ds(piece * tall, tall)]


def cross(left, left_in, partner, x_send, x_recv, piece):
    copy = remote(piece_of(left, piece), piece_of(left_in, piece), x_send.at[piece], x_recv.at[piece], partner)
    copy.start()
    return copy


def scatter_sum(left, left_in, crossing, base, out, w_own, w_other, boxes, up, down, y_pos):
    outbox, inbox, relay_out, relay_in, pending, kept, y_send, y_recv, r_send, r_recv = boxes
    rows, width = left.shape
    tall = rows // PIECES
    ways = (up, down)
    copies = []

    def term(piece, step):
        cols = pl.ds(pl.multiple_of(lax.rem(y_pos + step, N_Y) * width, width), width)
        part = pl.ds(piece * tall, tall)
        return (jnp.dot(left[part, :], w_own[:, cols], preferred_element_type=jnp.float32)
                + jnp.dot(left_in[part, :], w_other[:, cols], preferred_element_type=jnp.float32))

    def send(way, piece, value):
        outbox[way, piece] = value.astype(jnp.bfloat16)
        copy = remote(outbox.at[way, piece], inbox.at[way, piece], y_send.at[way, piece], y_recv.at[way, piece],
                      ways[way])
        copy.start()
        copies.append(copy)
        return copy

    arrivals = {}
    relays = []

    def combine(piece):
        relays[piece].wait_recv()
        way = piece % 2
        arrivals[way, piece] = send(way, piece, pending[piece] + relay_in[piece].astype(jnp.float32))

    for piece in range(PIECES):
        crossing[piece].wait_recv()
        way = piece % 2
        relay_out[piece] = term(piece, 2).astype(jnp.bfloat16)
        relay = remote(relay_out.at[piece], relay_in.at[piece], r_send.at[piece], r_recv.at[piece], ways[way])
        relay.start()
        relays.append(relay)
        arrivals[1 - way, piece] = send(1 - way, piece, term(piece, (1, 3)[1 - way]))
        pending[piece] = term(piece, (1, 3)[way])
        part = pl.ds(piece * tall, tall)
        kept[part, :] = term(piece, 0) + base[part, :].astype(jnp.float32)
        if piece:
            combine(piece - 1)
    combine(PIECES - 1)

    def finish():
        for piece in range(PIECES):
            part = pl.ds(piece * tall, tall)
            for way in (1 - piece % 2, piece % 2):
                arrivals[way, piece].wait_recv()
            total = kept[part, :] + inbox[0, piece].astype(jnp.float32) + inbox[1, piece].astype(jnp.float32)
            out[part, :] = total.astype(jnp.bfloat16)
        for copy in list(crossing) + copies + relays:
            copy.wait_send()

    return finish


def box_shapes(rows, width):
    tall = rows // PIECES
    dma = pltpu.SemaphoreType.DMA
    return [
        pltpu.VMEM((2, PIECES, tall, width), jnp.bfloat16),
        pltpu.VMEM((2, PIECES, tall, width), jnp.bfloat16),
        pltpu.VMEM((PIECES, tall, width), jnp.bfloat16),
        pltpu.VMEM((PIECES, tall, width), jnp.bfloat16),
        pltpu.VMEM((PIECES, tall, width), jnp.float32),
        pltpu.VMEM((rows, width), jnp.float32),
        dma((2, PIECES)), dma((2, PIECES)), dma((PIECES,)), dma((PIECES,)),
    ]


def project_kernel(left_ref, base_ref, own_ref, other_ref, out_ref, w_own, w_other, left_in, w_sem, x_send, x_recv,
                   *boxes):
    y_pos, x_lo, partner, up, down = column_places()
    span = w_own.shape[1]
    half = pl.ds(pl.multiple_of(x_lo * span, span), span)
    load_own = pltpu.make_async_copy(own_ref.at[:, half], w_own, w_sem.at[0])
    load_other = pltpu.make_async_copy(other_ref, w_other, w_sem.at[1])
    load_own.start()
    load_other.start()
    greet([partner, up, down])
    crossing = [cross(left_ref, left_in, partner, x_send, x_recv, piece) for piece in range(PIECES)]
    load_own.wait()
    load_other.wait()
    scatter_sum(left_ref, left_in, crossing, base_ref, out_ref, w_own, w_other, boxes, up, down, y_pos)()


def project(left, base, own_weight, other_half):
    rows, depth = left.shape
    dma = pltpu.SemaphoreType.DMA
    return pl.pallas_call(
        project_kernel,
        out_shape=jax.ShapeDtypeStruct((rows, depth), jnp.bfloat16),
        in_specs=whole(2) + [pl.BlockSpec(memory_space=pl.ANY)] * 2,
        out_specs=pl.BlockSpec(memory_space=pltpu.VMEM),
        scratch_shapes=[
            pltpu.VMEM((depth, N_Y * depth), jnp.bfloat16),
            pltpu.VMEM((depth, N_Y * depth), jnp.bfloat16),
            pltpu.VMEM((rows, depth), jnp.bfloat16),
            dma((2,)), dma((PIECES,)), dma((PIECES,)),
        ] + box_shapes(rows, depth),
        compiler_params=pltpu.CompilerParams(collective_id=4, has_side_effects=True, vmem_limit_bytes=VMEM_LIMIT),
        name="project",
    )(left, base, own_weight, other_half)


def hyena_kernel(feat_ref, short_ref, medium_ref, skip_ref, base_ref, first_weight, second_weight,
                 out_ref, second_half,
                 halo, ext, taps, product, product_t, query, mixed_t, send_sem, recv_sem,
                 w_own, first_half, gated, gated_in, w_sem, x_send, x_recv, g_send, g_recv,
                 w_send, w_recv, v_send, v_recv, *boxes):
    rows, chans = out_ref.shape
    ctx = lax.axis_index("ctx")
    chan = lax.axis_index("ch")
    after = (lax.rem(ctx + 1, N_CTX), chan)
    before = (lax.rem(ctx + N_CTX - 1, N_CTX), chan)
    y_pos, x_lo, partner, up, down = column_places()
    core, z_pos, sibling, ring = ring_z()
    span = first_half.shape[1]
    load_own = pltpu.make_async_copy(
        first_weight.at[:, pl.ds(pl.multiple_of(x_lo * span, span), span)], w_own, w_sem)
    load_own.start()
    greet([after, before, partner, sibling, up, down] + ring)
    near = remote(feat_ref.at[pl.ds(0, 1), pl.ds(rows - 16, 16)], halo.at[pl.ds(0, 1), pl.ds(HALO - 16, 16)],
                  send_sem.at[0], recv_sem.at[0], after)
    far = remote(feat_ref.at[pl.ds(1, 2), pl.ds(rows - HALO, HALO)], halo.at[pl.ds(1, 2)],
                 send_sem.at[1], recv_sem.at[1], after)
    near.start()
    far.start()
    tall = first_half.shape[0] // (2 * N_Z)
    mine = piece_rows(z_pos, core, tall)
    half = pl.ds(pl.multiple_of((1 - x_lo) * span, span), span)
    cross_first = remote(first_weight.at[mine, half], first_half.at[mine], x_send.at[0], x_recv.at[0], partner)
    cross_second = remote(second_weight.at[mine, half], second_half.at[mine], x_send.at[1], x_recv.at[1], partner)
    cross_first.start()
    cross_second.start()
    spread = Spread(first_half.at[mine], first_half, w_send, w_recv)
    later = Spread(second_half.at[mine], second_half, v_send, v_recv)

    groups = short_ref.shape[2]
    widen = (lax.broadcasted_iota(jnp.int32, (groups, chans), 1) // GROUP_SIZE
              == lax.broadcasted_iota(jnp.int32, (groups, chans), 0)).astype(jnp.float32)
    for kind in range(3):
        taps[kind, 0:7, :] = jnp.dot(short_ref[kind], widen, preferred_element_type=jnp.float32,
                                     precision=lax.Precision.HIGHEST)
        ext[kind, HALO:, :] = feat_ref[kind].astype(jnp.float32)

    def featured(kind, first, count):
        slab = ext[kind, pl.ds(first - 8 if isinstance(first, int) else pl.multiple_of(first - 8, 8), count + 8), :]
        total = taps[kind, 0:1, :] * slab[8:]
        for tap in range(1, 7):
            total = total + taps[kind, tap : tap + 1, :] * pltpu.roll(slab, tap, 0)[8:]
        return total

    def main_rows(step, carry):
        first = pl.multiple_of(16 + step * 16, 16)
        query[pl.ds(first, 16), :] = featured(0, pl.multiple_of(first + HALO, 16), 16)
        product[pl.ds(first + 128, 16), :] = featured(1, pl.multiple_of(first + HALO, 16), 16) * featured(2, pl.multiple_of(first + HALO, 16), 16)
        return carry

    lax.fori_loop(0, 16, main_rows, 0)
    cross_first.wait_recv()
    spread.first()
    lax.fori_loop(16, rows // 16 - 1, main_rows, 0)
    near.wait()
    far.wait()
    keep = (ctx > 0).astype(jnp.float32)
    ext[0, HALO - 16 : HALO, :] = halo[0, HALO - 16 : HALO, :].astype(jnp.float32) * keep
    for kind in (1, 2):
        ext[kind, 0:HALO, :] = halo[kind].astype(jnp.float32) * keep
    query[0:16, :] = featured(0, HALO, 16)

    def rim_rows(step, carry):
        first = pl.multiple_of(step * 16, 16)
        product[pl.ds(first, 16), :] = featured(1, pl.multiple_of(first + 16, 16), 16) * featured(2, pl.multiple_of(first + 16, 16), 16)
        return carry

    lax.fori_loop(0, 9, rim_rows, 0)
    for block in range(5):
        product_t[:, 128 * block : 128 * block + 128] = (
            product[128 * block : 128 * block + 128, :].T.astype(jnp.bfloat16))
    row = lax.broadcasted_iota(jnp.int32, (128, 128), 0)
    col = lax.broadcasted_iota(jnp.int32, (128, 128), 1)

    def one_group(group, carry):
        line = jnp.broadcast_to(medium_ref[pl.ds(group, 1), :], (128, 128))
        wheel = pltpu.roll(line, 0, 1, stride=1, stride_axis=0)
        table = jnp.concatenate([jnp.where(col < row, wheel, 0.0), jnp.where(col >= row, wheel, 0.0)],
                                axis=0).astype(jnp.bfloat16)
        lane = pl.ds(pl.multiple_of(group * GROUP_SIZE, GROUP_SIZE), GROUP_SIZE)
        window = jnp.concatenate(
            [product_t[lane, 128 * block : 128 * block + 256] for block in range(4)], axis=0)
        mix = jnp.dot(window, table, preferred_element_type=jnp.float32)
        for block in range(4):
            mixed_t[lane, 128 * block : 128 * block + 128] = mix[16 * block : 16 * block + 16, :]
        return carry

    lax.fori_loop(0, groups, one_group, 0)
    crossing = []
    for block in range(4):
        part = pl.ds(128 * block, 128)
        mix = mixed_t[:, part].T
        inner = product[pl.ds(128 * block + 128, 128), :].astype(jnp.bfloat16).astype(jnp.float32)
        gated[part, :] = (query[part, :] * (mix + skip_ref[...] * inner)).astype(jnp.bfloat16)
        crossing.append(cross(gated, gated_in, partner, g_send, g_recv, block))
    spread.second()
    cross_second.wait_recv()
    later.first()
    load_own.wait()
    spread.finish()
    finish = scatter_sum(gated, gated_in, crossing, base_ref, out_ref, w_own, first_half, boxes, up, down, y_pos)
    later.second()
    finish()
    cross_first.wait_send()
    cross_second.wait_send()
    later.finish()


def hyena(feats, short_filter, medium_t, skip_row, base, first_weight, second_weight):
    kinds, rows, chans = feats.shape
    deep, wide = first_weight.shape
    dma = pltpu.SemaphoreType.DMA
    anywhere = pl.BlockSpec(memory_space=pl.ANY)
    return pl.pallas_call(
        hyena_kernel,
        out_shape=(jax.ShapeDtypeStruct((rows, chans), jnp.bfloat16),
                   jax.ShapeDtypeStruct((deep, wide // 2), jnp.bfloat16)),
        in_specs=whole(5) + [anywhere] * 2,
        out_specs=(pl.BlockSpec(memory_space=pltpu.VMEM), anywhere),
        scratch_shapes=[
            pltpu.VMEM((3, HALO, chans), jnp.bfloat16),
            pltpu.VMEM((3, HALO + rows, chans), jnp.float32),
            pltpu.VMEM((3, 8, chans), jnp.float32),
            pltpu.VMEM((128 + rows, chans), jnp.float32),
            pltpu.VMEM((chans, 128 + rows), jnp.bfloat16),
            pltpu.VMEM((rows, chans), jnp.float32),
            pltpu.VMEM((chans, rows), jnp.float32),
            dma((2,)), dma((2,)),
            pltpu.VMEM((deep, wide // 2), jnp.bfloat16),
            pltpu.VMEM((deep, wide // 2), jnp.bfloat16),
            pltpu.VMEM((rows, chans), jnp.bfloat16),
            pltpu.VMEM((rows, chans), jnp.bfloat16),
            dma, dma((2,)), dma((2,)), dma((PIECES,)), dma((PIECES,)),
            dma((7,)), dma((7,)), dma((7,)), dma((7,)),
        ] + box_shapes(rows, chans),
        compiler_params=pltpu.CompilerParams(collective_id=0, has_side_effects=True, vmem_limit_bytes=VMEM_LIMIT),
        name="hyena",
    )(feats, short_filter, medium_t, skip_row, base, first_weight, second_weight)


def qkv_kernel(stream_ref, gain_ref, cos_ref, sin_ref, w_hbm, out_ref,
               blocks, w_ref, acc, squares, w_sem, send_sem, recv_sem):
    rows, width = stream_ref.shape
    ctx = lax.axis_index("ctx")
    chan = lax.axis_index("ch")
    y_pos = lax.rem(chan, N_Y)
    x_lo = chan // N_Y
    x_hi = 1 - x_lo
    up, down, opposite = lax.rem(y_pos + 1, N_Y), lax.rem(y_pos + 3, N_Y), lax.rem(y_pos + 2, N_Y)
    dev_up = (ctx, x_lo * N_Y + up)
    dev_down = (ctx, x_lo * N_Y + down)
    dev_x = (ctx, x_hi * N_Y + y_pos)
    load = pltpu.make_async_copy(w_hbm, w_ref, w_sem)
    load.start()
    greet([dev_up, dev_down, dev_x])
    tall = rows // 2
    halves = [pl.ds(0, tall), pl.ds(tall, tall)]

    def slot(x, y):
        return x * N_Y + y

    sent = {}

    def push(name, src, where, part, target):
        index = len(sent)
        copy = remote(src, blocks.at[where, part], send_sem.at[index], recv_sem.at[index], target)
        copy.start()
        sent[name] = copy

    mine = slot(x_lo, y_pos)
    for number, part in enumerate(halves):
        push(("x", number), stream_ref.at[part], mine, part, dev_x)
        push(("up", number), stream_ref.at[part], mine, part, dev_up)
        push(("down", number), stream_ref.at[part], mine, part, dev_down)

    load.wait()
    squares[...] = jnp.zeros_like(squares)

    def use(block, where, first):
        wide = block.astype(jnp.float32)
        square = wide * wide
        squares[...] += (square[:, 0:128] + square[:, 128:256]) + (square[:, 256:384] + square[:, 384:512])
        cols = pl.ds(pl.multiple_of(where * width, width), width)
        scaled = (wide * gain_ref[:, cols]).astype(jnp.bfloat16)
        term = jnp.dot(scaled, w_ref[cols, :], preferred_element_type=jnp.float32)
        acc[...] = term if first else acc[...] + term

    use(stream_ref[...], mine, True)
    sent["up", 0].wait_recv()
    push(("upup", 0), blocks.at[slot(x_lo, down), halves[0]], slot(x_lo, down), halves[0], dev_up)
    sent["down", 0].wait_recv()
    sent["down", 1].wait_recv()
    push(("downdown", 0), blocks.at[slot(x_lo, up), halves[1]], slot(x_lo, up), halves[1], dev_down)
    sent["x", 0].wait_recv()
    other = slot(x_hi, y_pos)
    push(("xup", 0), blocks.at[other, halves[0]], other, halves[0], dev_up)
    push(("xdown", 0), blocks.at[other, halves[0]], other, halves[0], dev_down)
    sent["x", 1].wait_recv()
    push(("xup", 1), blocks.at[other, halves[1]], other, halves[1], dev_up)
    push(("xdown", 1), blocks.at[other, halves[1]], other, halves[1], dev_down)
    use(blocks[slot(x_lo, up)], slot(x_lo, up), False)
    sent["upup", 0].wait_recv()
    far = slot(x_lo, opposite)
    push(("far", 0), blocks.at[far, halves[0]], far, halves[0], dev_x)
    sent["downdown", 0].wait_recv()
    push(("far", 1), blocks.at[far, halves[1]], far, halves[1], dev_x)
    sent["up", 1].wait_recv()
    use(blocks[slot(x_lo, down)], slot(x_lo, down), False)
    use(blocks[other], other, False)
    use(blocks[far], far, False)
    for name, y in (("xdown", up), ("xup", down), ("far", opposite)):
        sent[name, 0].wait_recv()
        sent[name, 1].wait_recv()
        use(blocks[slot(x_hi, y)], slot(x_hi, y), False)

    inverse = lax.rsqrt(jnp.sum(squares[...], axis=1, keepdims=True) / (N_CH * width) + norm_eps)
    scale = HEAD ** -0.5 * 1.4426950408889634
    for head in range(4):
        for kind in range(3):
            first = (head * 3 + kind) * HEAD
            value = acc[:, first : first + HEAD] * inverse
            if kind < 2:
                value = value * cos_ref[...] + pltpu.roll(value, HEAD // 2, 1) * sin_ref[...]
            if kind == 0:
                value = value * scale
            out_ref[head, kind] = value.astype(jnp.bfloat16)
    for copy in sent.values():
        copy.wait_send()


def gathered_qkv(stream, gain_row, cosine, sine, weight):
    rows, width = stream.shape
    heads = weight.shape[1] // (3 * HEAD)
    return pl.pallas_call(
        qkv_kernel,
        out_shape=jax.ShapeDtypeStruct((heads, 3, rows, HEAD), jnp.bfloat16),
        in_specs=whole(4) + [pl.BlockSpec(memory_space=pl.ANY)],
        out_specs=pl.BlockSpec(memory_space=pltpu.VMEM),
        scratch_shapes=[
            pltpu.VMEM((N_CH, rows, width), jnp.bfloat16),
            pltpu.VMEM(weight.shape, jnp.bfloat16),
            pltpu.VMEM((rows, weight.shape[1]), jnp.float32),
            pltpu.VMEM((rows, 128), jnp.float32),
            pltpu.SemaphoreType.DMA,
            pltpu.SemaphoreType.DMA((14,)),
            pltpu.SemaphoreType.DMA((14,)),
        ],
        compiler_params=pltpu.CompilerParams(collective_id=2, has_side_effects=True, vmem_limit_bytes=VMEM_LIMIT),
        name="gather_qkv",
    )(stream, gain_row, cosine, sine, weight)


def attention_kernel(qkv_ref, out_ref, queries, keyvals, acc, peak, outbox,
                     own_sem, q_send, q_recv, z_send, z_recv, s_send, s_recv,
                     h_send, h_recv, t_send, t_recv, o_send, o_recv):
    heads, kinds, rows, head = qkv_ref.shape
    ctx = lax.axis_index("ctx")
    chan = lax.axis_index("ch")
    core = lax.rem(ctx, 2)
    z_pos = lax.rem(ctx // 2, N_Z)
    high = ctx // (2 * N_Z)

    def place(x, z, c):
        return ((x * N_Z + z) * 2 + c, chan)

    sibling = place(high, z_pos, 1 - core)
    across = place(1 - high, z_pos, core)
    ring = [place(high, lax.rem(z_pos + step, N_Z), core) for step in range(1, N_Z)]
    greet(ring + [sibling, across])

    def source(step):
        return lax.rem(z_pos + N_Z - step, N_Z)

    own_q = pltpu.make_async_copy(qkv_ref.at[z_pos, 0], queries.at[z_pos], own_sem.at[0])
    own_kv = pltpu.make_async_copy(qkv_ref.at[z_pos, pl.ds(1, 2)], keyvals.at[high, z_pos, :, core], own_sem.at[1])
    own_kv.start()
    own_q.start()
    z_copies, q_copies = [], []
    for step in (1, 2, 3):
        target = lax.rem(z_pos + step, N_Z)
        copy = remote(qkv_ref.at[target, pl.ds(1, 2)], keyvals.at[high, z_pos, :, core],
                      z_send.at[step - 1], z_recv.at[step - 1], ring[step - 1])
        copy.start()
        z_copies.append(copy)
    for step in (1, 2, 3):
        target = lax.rem(z_pos + step, N_Z)
        copy = remote(qkv_ref.at[target, 0], queries.at[z_pos],
                      q_send.at[step - 1], q_recv.at[step - 1], ring[step - 1])
        copy.start()
        q_copies.append(copy)
    shares, hops = [], []

    def spread(step):
        place_here = keyvals.at[high, source(step), :, core]
        share = remote(place_here, place_here, s_send.at[step], s_recv.at[step], sibling)
        share.start()
        shares.append(share)
        hop = remote(place_here, place_here, h_send.at[step], h_recv.at[step], across)
        hops.append(hop)

        @pl.when(high == 0)
        def _():
            hop.start()

    own_kv.wait()
    spread(0)
    for step in (1, 3, 2):
        z_copies[step - 1].wait_recv()
        spread(step)
    own_q.wait()
    for copy in q_copies:
        copy.wait_recv()
    for share in shares:
        share.wait_recv()

    tile = 128
    span = 2 * rows
    row = lax.broadcasted_iota(jnp.int32, (tile, span), 0) + core * rows
    col = lax.broadcasted_iota(jnp.int32, (tile, span), 1)
    ones = jnp.ones((span, head), jnp.bfloat16)

    def update(block, x, z, diagonal):
        keys = keyvals[x, z, 0].reshape(span, head)
        values = jnp.concatenate([keyvals[x, z, 1].reshape(span, head), ones], axis=1)
        for first in range(0, rows, tile):
            part = pl.ds(first, tile)
            scores = lax.dot_general(queries[block, part], keys, (((1,), (1,)), ((), ())),
                                     preferred_element_type=jnp.float32)
            if diagonal:
                scores = jnp.where(col <= row + first, scores, -1e30)
            top = jnp.max(scores, axis=1, keepdims=True)
            if diagonal:
                new = jnp.broadcast_to(top, (tile, head))
            else:
                old = peak[block, part]
                new = jnp.maximum(old, top)
                shrink = jnp.exp2(old - new)
            peak[block, part] = new
            weights = jnp.exp2(scores - jnp.concatenate([new] * (span // head), axis=1)).astype(jnp.bfloat16)
            term = jnp.dot(weights, values, preferred_element_type=jnp.float32)
            if not diagonal:
                term = acc[block, part] * jnp.concatenate([shrink, shrink], axis=1) + term
            acc[block, part] = term

    lanes = pl.ds(pl.multiple_of(z_pos * head, head), head)

    def result_copy(block):
        return remote(outbox.at[block], out_ref.at[:, lanes], o_send.at[block],
                      o_recv.at[z_pos], place(high, block, core))

    def complete(block):
        result = acc[block]
        outbox[block] = (result[:, :head] / result[:, head:]).astype(jnp.bfloat16)

        @pl.when(block != z_pos)
        def _():
            result_copy(block).start()

        @pl.when(block == z_pos)
        def _():
            out_ref[:, lanes] = outbox[block]

    def own_part(block, carry):
        update(block, high, block, True)

        def earlier(z, inner):
            update(block, high, z, False)
            return inner

        lax.fori_loop(0, block, earlier, 0)

        @pl.when(high == 0)
        def _():
            complete(block)

        return carry

    lax.fori_loop(0, N_Z, own_part, 0)

    @pl.when(high == 1)
    def _():
        passes = []
        for order, step in enumerate((0, 1, 3, 2)):
            hops[order].wait_recv()
            landed = keyvals.at[0, source(step), :, core]
            copy = remote(landed, landed, t_send.at[step], t_recv.at[step], sibling)
            copy.start()
            passes.append(copy)
        for copy in passes:
            copy.wait_recv()

        def low_part(block, carry):
            def each(z, inner):
                update(block, 0, z, False)
                return inner

            lax.fori_loop(0, N_Z, each, 0)
            complete(block)
            return carry

        lax.fori_loop(0, N_Z, low_part, 0)
        for copy in passes:
            copy.wait_send()

    for step in (1, 3, 2):
        other = lax.rem(z_pos + step, N_Z)
        landing = pl.ds(pl.multiple_of(other * head, head), head)
        remote(outbox.at[other], out_ref.at[:, landing], o_send.at[other], o_recv.at[other],
               place(high, other, core)).wait()
    for copy in z_copies + q_copies + shares:
        copy.wait_send()

    @pl.when(high == 0)
    def _():
        for hop in hops:
            hop.wait_send()


def attention(qkv):
    heads, kinds, rows, head = qkv.shape
    dma = pltpu.SemaphoreType.DMA
    return pl.pallas_call(
        attention_kernel,
        out_shape=jax.ShapeDtypeStruct((rows, heads * head), jnp.bfloat16),
        in_specs=whole(1),
        out_specs=pl.BlockSpec(memory_space=pltpu.VMEM),
        scratch_shapes=[
            pltpu.VMEM((N_Z, rows, head), jnp.bfloat16),
            pltpu.VMEM((2, N_Z, 2, 2, rows, head), jnp.bfloat16),
            pltpu.VMEM((N_Z, rows, 2 * head), jnp.float32),
            pltpu.VMEM((N_Z, rows, head), jnp.float32),
            pltpu.VMEM((N_Z, rows, head), jnp.bfloat16),
            dma((2,)), dma((3,)), dma((3,)), dma((3,)), dma((3,)), dma((4,)), dma((4,)),
            dma((4,)), dma((4,)), dma((4,)), dma((4,)), dma((4,)), dma((4,)),
        ],
        compiler_params=pltpu.CompilerParams(collective_id=3, has_side_effects=True, vmem_limit_bytes=VMEM_LIMIT),
        name="attention",
    )(qkv)


def rotation_tables(rows):
    positions = lax.axis_index("ctx") * rows + jnp.arange(rows, dtype=jnp.int32)
    half_size = HEAD // 2
    frequency = 10000.0 ** (-jnp.arange(half_size, dtype=jnp.float32) * 2.0 / HEAD)
    angles = positions.astype(jnp.float32)[:, None] * frequency[None, :]
    cosine, sine = jnp.cos(angles), jnp.sin(angles)
    return jnp.concatenate([cosine, cosine], axis=1), jnp.concatenate([-sine, sine], axis=1)


def shards(features, residual_in, short_filter, medium_filter, skip_gain, out_weight, norm_gain, attn_weight,
           attn_out):
    rows = features.shape[0]
    cosine, sine = rotation_tables(rows)
    stream, attn_half = hyena(jnp.transpose(features, (1, 0, 2)), short_filter, medium_filter.T,
                              skip_gain[None, :], residual_in, out_weight, attn_out)
    qkv = gathered_qkv(stream, norm_gain[None, :], cosine, sine, attn_weight)
    attended = attention(qkv)
    return project(attended, stream, attn_out, attn_half)


def solution(mesh):
    in_specs = (
        P("ctx", None, "ch"),
        P("ctx", "ch"),
        P(None, None, "ch"),
        P(None, "ch"),
        P("ch"),
        P("ch", None),
        P(),
        P(None, "ch"),
        P("ch", None),
    )
    out_specs = P("ctx", "ch")
    return jax.shard_map(shards, mesh=mesh, in_specs=in_specs, out_specs=out_specs, check_vma=False)
```

```python
import functools

import jax
import jax.numpy as jnp
from jax import lax
from jax.experimental import pallas as pl
from jax.experimental.pallas import tpu as pltpu
from jax.sharding import PartitionSpec as P

HEAD = 128
GROUP_SIZE = 16
N_CH = 8
N_CTX = 16
N_Y = 4
N_Z = 4
HALO = 144

norm_eps = 1e-05
MESH = pl.DeviceIdType.MESH
VMEM_LIMIT = 60 * 1024 * 1024


def remote(src, dst, send_sem, recv_sem, target):
    return pltpu.make_async_remote_copy(
        src_ref=src, dst_ref=dst, send_sem=send_sem, recv_sem=recv_sem,
        device_id=target, device_id_type=MESH,
    )


def greet(targets):
    barrier = pltpu.get_barrier_semaphore()
    for target in targets:
        pl.semaphore_signal(barrier, inc=1, device_id=target, device_id_type=MESH)
    pl.semaphore_wait(barrier, len(targets))


def whole(count):
    return [pl.BlockSpec(memory_space=pltpu.VMEM)] * count


def ring_z():
    ctx = lax.axis_index("ctx")
    chan = lax.axis_index("ch")
    core = lax.rem(ctx, 2)
    z_pos = lax.rem(ctx // 2, N_Z)
    base = ctx - z_pos * 2 - core
    sibling = (base + z_pos * 2 + 1 - core, chan)
    ring = [(base + lax.rem(z_pos + step, N_Z) * 2 + core, chan) for step in range(1, N_Z)]
    return core, z_pos, sibling, ring


def piece_rows(z_pos, core, tall):
    return pl.ds(pl.multiple_of((z_pos * 2 + core) * tall, tall), tall)


class Spread:
    def __init__(self, piece_ref, whole_ref, send_sem, recv_sem):
        self.piece, self.whole = piece_ref, whole_ref
        self.send, self.recv = send_sem, recv_sem
        self.core, self.z_pos, self.sibling, self.ring = ring_z()
        self.tall = whole_ref.shape[0] // (2 * N_Z)
        self.copies = []

    def push(self, src, rows, target):
        index = len(self.copies)
        copy = remote(src, self.whole.at[rows], self.send.at[index], self.recv.at[index], target)
        copy.start()
        self.copies.append(copy)

    def first(self):
        rows = piece_rows(self.z_pos, self.core, self.tall)
        for target in self.ring + [self.sibling]:
            self.push(self.piece, rows, target)

    def second(self):
        for step in (1, 3, 2):
            self.copies[step - 1].wait_recv()
            rows = piece_rows(lax.rem(self.z_pos + N_Z - step, N_Z), self.core, self.tall)
            self.push(self.whole.at[rows], rows, self.sibling)

    def finish(self):
        for copy in self.copies[3:]:
            copy.wait_recv()
        for copy in self.copies:
            copy.wait_send()


PIECES = 4


def column_places():
    ctx = lax.axis_index("ctx")
    chan = lax.axis_index("ch")
    y_pos = lax.rem(chan, N_Y)
    x_lo = chan // N_Y
    partner = (ctx, (1 - x_lo) * N_Y + y_pos)
    up = (ctx, x_lo * N_Y + lax.rem(y_pos + 1, N_Y))
    down = (ctx, x_lo * N_Y + lax.rem(y_pos + 3, N_Y))
    return y_pos, x_lo, partner, up, down


def piece_of(ref, piece):
    tall = ref.shape[0] // PIECES
    return ref.at[pl.ds(piece * tall, tall)]


def cross(left, left_in, partner, x_send, x_recv, piece):
    copy = remote(piece_of(left, piece), piece_of(left_in, piece), x_send.at[piece], x_recv.at[piece], partner)
    copy.start()
    return copy


def scatter_sum(left, left_in, crossing, base, out, w_own, w_other, boxes, up, down, y_pos):
    outbox, inbox, relay_out, relay_in, pending, kept, y_send, y_recv, r_send, r_recv = boxes
    rows, width = left.shape
    tall = rows // PIECES
    ways = (up, down)
    copies = []

    def term(piece, step):
        cols = pl.ds(pl.multiple_of(lax.rem(y_pos + step, N_Y) * width, width), width)
        part = pl.ds(piece * tall, tall)
        return (jnp.dot(left[part, :], w_own[:, cols], preferred_element_type=jnp.float32)
                + jnp.dot(left_in[part, :], w_other[:, cols], preferred_element_type=jnp.float32))

    def send(way, piece, value):
        outbox[way, piece] = value.astype(jnp.bfloat16)
        copy = remote(outbox.at[way, piece], inbox.at[way, piece], y_send.at[way, piece], y_recv.at[way, piece],
                      ways[way])
        copy.start()
        copies.append(copy)
        return copy

    arrivals = {}
    relays = []

    def combine(piece):
        relays[piece].wait_recv()
        way = piece % 2
        arrivals[way, piece] = send(way, piece, pending[piece] + relay_in[piece].astype(jnp.float32))

    for piece in range(PIECES):
        crossing[piece].wait_recv()
        way = piece % 2
        relay_out[piece] = term(piece, 2).astype(jnp.bfloat16)
        relay = remote(relay_out.at[piece], relay_in.at[piece], r_send.at[piece], r_recv.at[piece], ways[way])
        relay.start()
        relays.append(relay)
        arrivals[1 - way, piece] = send(1 - way, piece, term(piece, (1, 3)[1 - way]))
        pending[piece] = term(piece, (1, 3)[way])
        part = pl.ds(piece * tall, tall)
        kept[part, :] = term(piece, 0) + base[part, :].astype(jnp.float32)
        if piece:
            combine(piece - 1)
    combine(PIECES - 1)

    def finish():
        for piece in range(PIECES):
            part = pl.ds(piece * tall, tall)
            for way in (1 - piece % 2, piece % 2):
                arrivals[way, piece].wait_recv()
            total = kept[part, :] + inbox[0, piece].astype(jnp.float32) + inbox[1, piece].astype(jnp.float32)
            out[part, :] = total.astype(jnp.bfloat16)
        for copy in list(crossing) + copies + relays:
            copy.wait_send()

    return finish


def box_shapes(rows, width):
    tall = rows // PIECES
    dma = pltpu.SemaphoreType.DMA
    return [
        pltpu.VMEM((2, PIECES, tall, width), jnp.bfloat16),
        pltpu.VMEM((2, PIECES, tall, width), jnp.bfloat16),
        pltpu.VMEM((PIECES, tall, width), jnp.bfloat16),
        pltpu.VMEM((PIECES, tall, width), jnp.bfloat16),
        pltpu.VMEM((PIECES, tall, width), jnp.float32),
        pltpu.VMEM((rows, width), jnp.float32),
        dma((2, PIECES)), dma((2, PIECES)), dma((PIECES,)), dma((PIECES,)),
    ]


def hyena_kernel(feat_ref, short_ref, medium_ref, skip_ref, base_ref, first_weight, second_weight,
                 out_ref, second_half,
                 halo, ext, taps, product, product_t, query, mixed_t, send_sem, recv_sem,
                 w_own, first_half, gated, gated_in, w_sem, x_send, x_recv, g_send, g_recv,
                 w_send, w_recv, v_send, v_recv, *boxes):
    rows, chans = out_ref.shape
    ctx = lax.axis_index("ctx")
    chan = lax.axis_index("ch")
    after = (lax.rem(ctx + 1, N_CTX), chan)
    before = (lax.rem(ctx + N_CTX - 1, N_CTX), chan)
    y_pos, x_lo, partner, up, down = column_places()
    core, z_pos, sibling, ring = ring_z()
    span = first_half.shape[1]
    load_own = pltpu.make_async_copy(
        first_weight.at[:, pl.ds(pl.multiple_of(x_lo * span, span), span)], w_own, w_sem)
    load_own.start()
    greet([after, before, partner, sibling, up, down] + ring)
    near = remote(feat_ref.at[pl.ds(0, 1), pl.ds(rows - 16, 16)], halo.at[pl.ds(0, 1), pl.ds(HALO - 16, 16)],
                  send_sem.at[0], recv_sem.at[0], after)
    far = remote(feat_ref.at[pl.ds(1, 2), pl.ds(rows - HALO, HALO)], halo.at[pl.ds(1, 2)],
                 send_sem.at[1], recv_sem.at[1], after)
    near.start()
    far.start()
    tall = first_half.shape[0] // (2 * N_Z)
    mine = piece_rows(z_pos, core, tall)
    half = pl.ds(pl.multiple_of((1 - x_lo) * span, span), span)
    cross_first = remote(first_weight.at[mine, half], first_half.at[mine], x_send.at[0], x_recv.at[0], partner)
    cross_second = remote(second_weight.at[mine, half], second_half.at[mine], x_send.at[1], x_recv.at[1], partner)
    cross_first.start()
    spread = Spread(first_half.at[mine], first_half, w_send, w_recv)
    later = Spread(second_half.at[mine], second_half, v_send, v_recv)

    groups = short_ref.shape[2]
    widen = (lax.broadcasted_iota(jnp.int32, (groups, chans), 1) // GROUP_SIZE
              == lax.broadcasted_iota(jnp.int32, (groups, chans), 0)).astype(jnp.float32)
    for kind in range(3):
        taps[kind, 0:7, :] = jnp.dot(short_ref[kind], widen, preferred_element_type=jnp.float32,
                                     precision=lax.Precision.HIGHEST)
        ext[kind, HALO:, :] = feat_ref[kind].astype(jnp.float32)

    def featured(kind, first, count):
        slab = ext[kind, pl.ds(first - 8 if isinstance(first, int) else pl.multiple_of(first - 8, 8), count + 8), :]
        total = taps[kind, 0:1, :] * slab[8:]
        for tap in range(1, 7):
            total = total + taps[kind, tap : tap + 1, :] * pltpu.roll(slab, tap, 0)[8:]
        return total

    def main_rows(step, carry):
        first = pl.multiple_of(16 + step * 16, 16)
        query[pl.ds(first, 16), :] = featured(0, pl.multiple_of(first + HALO, 16), 16)
        product[pl.ds(first + 128, 16), :] = featured(1, pl.multiple_of(first + HALO, 16), 16) * featured(2, pl.multiple_of(first + HALO, 16), 16)
        return carry

    lax.fori_loop(0, 8, main_rows, 0)
    cross_first.wait_recv()
    spread.first()
    cross_second.start()
    lax.fori_loop(8, rows // 16 - 1, main_rows, 0)
    near.wait()
    far.wait()
    keep = (ctx > 0).astype(jnp.float32)
    ext[0, HALO - 16 : HALO, :] = halo[0, HALO - 16 : HALO, :].astype(jnp.float32) * keep
    for kind in (1, 2):
        ext[kind, 0:HALO, :] = halo[kind].astype(jnp.float32) * keep
    query[0:16, :] = featured(0, HALO, 16)

    def rim_rows(step, carry):
        first = pl.multiple_of(step * 16, 16)
        product[pl.ds(first, 16), :] = featured(1, pl.multiple_of(first + 16, 16), 16) * featured(2, pl.multiple_of(first + 16, 16), 16)
        return carry

    lax.fori_loop(0, 9, rim_rows, 0)
    for block in range(5):
        product_t[:, 128 * block : 128 * block + 128] = (
            product[128 * block : 128 * block + 128, :].T.astype(jnp.bfloat16))
    row = lax.broadcasted_iota(jnp.int32, (128, 128), 0)
    col = lax.broadcasted_iota(jnp.int32, (128, 128), 1)

    def one_group(group, carry):
        line = jnp.broadcast_to(medium_ref[pl.ds(group, 1), :], (128, 128))
        wheel = pltpu.roll(line, 0, 1, stride=1, stride_axis=0)
        table = jnp.concatenate([jnp.where(col < row, wheel, 0.0), jnp.where(col >= row, wheel, 0.0)],
                                axis=0).astype(jnp.bfloat16)
        lane = pl.ds(pl.multiple_of(group * GROUP_SIZE, GROUP_SIZE), GROUP_SIZE)
        window = jnp.concatenate(
            [product_t[lane, 128 * block : 128 * block + 256] for block in range(4)], axis=0)
        mix = jnp.dot(window, table, preferred_element_type=jnp.float32)
        for block in range(4):
            mixed_t[lane, 128 * block : 128 * block + 128] = mix[16 * block : 16 * block + 16, :]
        return carry

    lax.fori_loop(0, groups, one_group, 0)
    crossing = []
    for block in range(4):
        part = pl.ds(128 * block, 128)
        mix = mixed_t[:, part].T
        inner = product[pl.ds(128 * block + 128, 128), :].astype(jnp.bfloat16).astype(jnp.float32)
        gated[part, :] = (query[part, :] * (mix + skip_ref[...] * inner)).astype(jnp.bfloat16)
        crossing.append(cross(gated, gated_in, partner, g_send, g_recv, block))
    spread.second()
    cross_second.wait_recv()
    later.first()
    load_own.wait()
    spread.finish()
    finish = scatter_sum(gated, gated_in, crossing, base_ref, out_ref, w_own, first_half, boxes, up, down, y_pos)
    later.second()
    finish()
    cross_first.wait_send()
    cross_second.wait_send()
    later.finish()


def hyena(feats, short_filter, medium_t, skip_row, base, first_weight, second_weight):
    kinds, rows, chans = feats.shape
    deep, wide = first_weight.shape
    dma = pltpu.SemaphoreType.DMA
    anywhere = pl.BlockSpec(memory_space=pl.ANY)
    return pl.pallas_call(
        hyena_kernel,
        out_shape=(jax.ShapeDtypeStruct((rows, chans), jnp.bfloat16),
                   jax.ShapeDtypeStruct((deep, wide // 2), jnp.bfloat16)),
        in_specs=whole(5) + [anywhere] * 2,
        out_specs=(pl.BlockSpec(memory_space=pltpu.VMEM), anywhere),
        scratch_shapes=[
            pltpu.VMEM((3, HALO, chans), jnp.bfloat16),
            pltpu.VMEM((3, HALO + rows, chans), jnp.float32),
            pltpu.VMEM((3, 8, chans), jnp.float32),
            pltpu.VMEM((128 + rows, chans), jnp.float32),
            pltpu.VMEM((chans, 128 + rows), jnp.bfloat16),
            pltpu.VMEM((rows, chans), jnp.float32),
            pltpu.VMEM((chans, rows), jnp.float32),
            dma((2,)), dma((2,)),
            pltpu.VMEM((deep, wide // 2), jnp.bfloat16),
            pltpu.VMEM((deep, wide // 2), jnp.bfloat16),
            pltpu.VMEM((rows, chans), jnp.bfloat16),
            pltpu.VMEM((rows, chans), jnp.bfloat16),
            dma, dma((2,)), dma((2,)), dma((PIECES,)), dma((PIECES,)),
            dma((7,)), dma((7,)), dma((7,)), dma((7,)),
        ] + box_shapes(rows, chans),
        compiler_params=pltpu.CompilerParams(collective_id=0, has_side_effects=True, vmem_limit_bytes=VMEM_LIMIT),
        name="hyena",
    )(feats, short_filter, medium_t, skip_row, base, first_weight, second_weight)


def attention_kernel(stream_ref, gain_ref, cos_ref, sin_ref, weight_ref, own_ref, other_ref, out_ref,
                     blocks, w_ref, wide_acc, squares, qkv,
                     queries, keyvals, acc, peak, results, attended, attended_in, w_own, w_other,
                     outbox, inbox, relay_out, relay_in, pending, kept,
                     y_send, y_recv, r_send, r_recv,
                     w_sem, g_send, g_recv, own_sem, q_send, q_recv, z_send, z_recv, s_send, s_recv,
                     h_send, h_recv, t_send, t_recv, o_send, o_recv, p_send, p_recv):
    rows, width = stream_ref.shape
    head = HEAD
    heads = width // head
    tile = rows // PIECES
    tall = rows // 2
    ctx = lax.axis_index("ctx")
    core = lax.rem(ctx, 2)
    z_pos = lax.rem(ctx // 2, N_Z)
    high = ctx // (2 * N_Z)
    chan = lax.axis_index("ch")
    y_pos, x_lo, partner, dev_up, dev_down = column_places()
    up, down, opposite = lax.rem(y_pos + 1, N_Y), lax.rem(y_pos + 3, N_Y), lax.rem(y_pos + 2, N_Y)
    wide = w_own.shape[1]
    loads = [
        pltpu.make_async_copy(weight_ref, w_ref, w_sem.at[0]),
        pltpu.make_async_copy(own_ref.at[:, pl.ds(pl.multiple_of(x_lo * wide, wide), wide)], w_own, w_sem.at[1]),
        pltpu.make_async_copy(other_ref, w_other, w_sem.at[2]),
    ]
    for load in loads:
        load.start()

    def place(x, z, c):
        return ((x * N_Z + z) * 2 + c, chan)

    def partner_place(z):
        return ((high * N_Z + z) * 2 + core, (1 - x_lo) * N_Y + y_pos)

    sibling = place(high, z_pos, 1 - core)
    across = place(1 - high, z_pos, core)
    others = [lax.rem(z_pos + step, N_Z) for step in range(1, N_Z)]
    ring = [place(high, z, core) for z in others]
    greet([dev_up, dev_down, partner, sibling, across] + ring + [partner_place(z) for z in others])

    def slot(x, y):
        return x * N_Y + y

    halves = [pl.ds(0, tall), pl.ds(tall, tall)]
    quarters = [[pl.ds(half * tall + number * (tall // 2), tall // 2) for number in range(2)] for half in range(2)]
    sent = {}

    def push(name, src, where, part, target):
        index = len(sent)
        copy = remote(src.at[part], blocks.at[where, part], g_send.at[index], g_recv.at[index], target)
        copy.start()
        sent[name] = copy

    mine, other = slot(x_lo, y_pos), slot(1 - x_lo, y_pos)
    above, below, far = slot(x_lo, up), slot(x_lo, down), slot(x_lo, opposite)

    def own_sends(half):
        part = halves[half]
        push(("x", half), stream_ref, mine, part, partner)
        push(("up", half), stream_ref, mine, part, dev_up)
        push(("down", half), stream_ref, mine, part, dev_down)

    def pass_on(half):
        first, second = quarters[half]
        part = halves[half]
        sent["up", half].wait_recv()
        push(("upup", half), blocks.at[below], below, first, dev_up)
        sent["down", half].wait_recv()
        push(("downdown", half), blocks.at[above], above, second, dev_down)
        sent["x", half].wait_recv()
        push(("xup", half), blocks.at[other], other, part, dev_up)
        push(("xdown", half), blocks.at[other], other, part, dev_down)

    def pass_far(half):
        first, second = quarters[half]
        sent["upup", half].wait_recv()
        push(("far0", half), blocks.at[far], far, first, partner)
        sent["downdown", half].wait_recv()
        push(("far1", half), blocks.at[far], far, second, partner)

    def use(src, where, half, fresh=False):
        part = halves[half]
        value = src[part, :].astype(jnp.float32)
        square = value * value
        partial = (square[:, 0:128] + square[:, 128:256]) + (square[:, 256:384] + square[:, 384:512])
        cols = pl.ds(pl.multiple_of(where * width, width), width)
        scaled = (value * gain_ref[:, cols]).astype(jnp.bfloat16)
        term = jnp.dot(scaled, w_ref[cols, :], preferred_element_type=jnp.float32)
        squares[part, :] = partial if fresh else squares[part, :] + partial
        wide_acc[part, :] = term if fresh else wide_acc[part, :] + term

    def last_uses(half):
        for names, y in ((("xdown",), up), (("xup",), down), (("far0", "far1"), opposite)):
            for name in names:
                sent[name, half].wait_recv()
            use(blocks.at[slot(1 - x_lo, y)], slot(1 - x_lo, y), half)

    scale = head ** -0.5 * 1.4426950408889634

    def heads_out(half):
        part = halves[half]
        inverse = lax.rsqrt(jnp.sum(squares[part, :], axis=1, keepdims=True) / (N_CH * width) + norm_eps)
        for number in range(heads):
            for kind in range(3):
                first = (number * 3 + kind) * head
                value = wide_acc[part, first : first + head] * inverse
                if kind < 2:
                    value = value * cos_ref[part, :] + pltpu.roll(value, head // 2, 1) * sin_ref[part, :]
                if kind == 0:
                    value = value * scale
                qkv[number, kind, part, :] = value.astype(jnp.bfloat16)

    z_copies, q_copies, own_copies = {}, {}, []

    def exchange(half):
        part = halves[half]
        own_kv = pltpu.make_async_copy(qkv.at[z_pos, pl.ds(1, 2), part],
                                       keyvals.at[high, z_pos, :, core, part], own_sem.at[half, 1])
        own_q = pltpu.make_async_copy(qkv.at[z_pos, 0, part], queries.at[z_pos, part], own_sem.at[half, 0])
        own_kv.start()
        own_q.start()
        own_copies.append((own_kv, own_q))
        for step in (1, 2, 3):
            copy = remote(qkv.at[others[step - 1], pl.ds(1, 2), part], keyvals.at[high, z_pos, :, core, part],
                          z_send.at[half, step - 1], z_recv.at[half, step - 1], ring[step - 1])
            copy.start()
            z_copies[half, step] = copy
        for step in (1, 2, 3):
            copy = remote(qkv.at[others[step - 1], 0, part], queries.at[z_pos, part],
                          q_send.at[half, step - 1], q_recv.at[half, step - 1], ring[step - 1])
            copy.start()
            q_copies[half, step] = copy

    own_sends(0)
    loads[0].wait()
    use(stream_ref, mine, 0, True)
    pass_on(0)
    own_sends(1)
    use(blocks.at[above], above, 0)
    use(blocks.at[below], below, 0)
    use(blocks.at[other], other, 0)
    pass_far(0)
    use(blocks.at[far], far, 0)
    use(stream_ref, mine, 1, True)
    last_uses(0)
    heads_out(0)
    exchange(0)
    pass_on(1)
    use(blocks.at[above], above, 1)
    use(blocks.at[below], below, 1)
    pass_far(1)
    use(blocks.at[other], other, 1)
    use(blocks.at[far], far, 1)
    last_uses(1)
    heads_out(1)
    exchange(1)

    def source(step):
        return lax.rem(z_pos + N_Z - step, N_Z)

    shares, hops = [], []

    def spread(step, half):
        index = len(shares)
        place_here = keyvals.at[high, source(step), :, core, halves[half]]
        share = remote(place_here, place_here, s_send.at[index], s_recv.at[index], sibling)
        share.start()
        shares.append(share)
        hop = remote(place_here, place_here, h_send.at[index], h_recv.at[index], across)
        hops.append(hop)

        @pl.when(high == 0)
        def _():
            hop.start()

    order = [(step, half) for half in range(2) for step in (0, 1, 3, 2)]
    for step, half in order:
        if step:
            z_copies[half, step].wait_recv()
        else:
            own_copies[half][0].wait()
        spread(step, half)
    for pair in own_copies:
        pair[1].wait()
    for copy in list(q_copies.values()) + shares:
        copy.wait_recv()

    span = 2 * rows
    row = lax.broadcasted_iota(jnp.int32, (tile, span), 0) + core * rows
    col = lax.broadcasted_iota(jnp.int32, (tile, span), 1)
    ones = jnp.ones((span, head), jnp.bfloat16)

    def piece_at(piece):
        return pl.ds(pl.multiple_of(piece * tile, tile), tile)

    def update(block, part, first, x, z, diagonal):
        keys = keyvals[x, z, 0].reshape(span, head)
        values = jnp.concatenate([keyvals[x, z, 1].reshape(span, head), ones], axis=1)
        scores = lax.dot_general(queries[block, part], keys, (((1,), (1,)), ((), ())),
                                 preferred_element_type=jnp.float32)
        if diagonal:
            scores = jnp.where(col <= row + first, scores, -1e30)
        top = jnp.max(scores, axis=1, keepdims=True)
        if diagonal:
            new = jnp.broadcast_to(top, (tile, head))
        else:
            old = peak[block, part]
            new = jnp.maximum(old, top)
            shrink = jnp.exp2(old - new)
        peak[block, part] = new
        weights = jnp.exp2(scores - jnp.concatenate([new] * (span // head), axis=1)).astype(jnp.bfloat16)
        term = jnp.dot(weights, values, preferred_element_type=jnp.float32)
        if not diagonal:
            term = acc[block, part] * jnp.concatenate([shrink, shrink], axis=1) + term
        acc[block, part] = term

    def own_tile(piece):
        part, first = piece_at(piece), piece * tile
        for block in range(N_Z):
            update(block, part, first, high, block, True)
        for z in range(N_Z - 1):
            for block in range(z + 1, N_Z):
                update(block, part, first, high, z, False)

    def low_tile(piece):
        part, first = piece_at(piece), piece * tile

        def each(z, carry):
            for block in range(N_Z):
                update(block, part, first, 0, z, False)
            return carry

        lax.fori_loop(0, N_Z, each, 0)

    lanes = pl.ds(pl.multiple_of(z_pos * head, head), head)

    def result_copy(piece, block, owner):
        columns = pl.ds(pl.multiple_of(owner * head, head), head)
        part = piece_at(piece)
        return remote(results.at[block, part], attended.at[part, columns], o_send.at[piece, block],
                      o_recv.at[piece, owner], place(high, block, core))

    def partner_copy(piece, block, owner):
        columns = pl.ds(pl.multiple_of(owner * head, head), head)
        part = piece_at(piece)
        return remote(results.at[block, part], attended_in.at[part, columns], p_send.at[piece, block],
                      p_recv.at[piece, owner], partner_place(block))

    def complete(piece):
        part = piece_at(piece)

        def each(block, carry):
            total = acc[block, part]
            results[block, part] = (total[:, :head] / total[:, head:]).astype(jnp.bfloat16)
            partner_copy(piece, block, z_pos).start()

            @pl.when(block != z_pos)
            def _():
                result_copy(piece, block, z_pos).start()

            @pl.when(block == z_pos)
            def _():
                attended[part, lanes] = results[block, part]

            return carry

        lax.fori_loop(0, N_Z, each, 0)

    def way_place(way):
        return (ctx, x_lo * N_Y + lax.rem(y_pos + 1 + 2 * way, N_Y))

    def relay_copy(piece):
        return remote(relay_out.at[piece], relay_in.at[piece], r_send.at[piece], r_recv.at[piece],
                      way_place(lax.rem(piece, 2)))

    def direct_copy(way, piece):
        return remote(outbox.at[way, piece], inbox.at[way, piece], y_send.at[way, piece], y_recv.at[way, piece],
                      way_place(way))

    def multiply(piece):
        for z in others:
            result_copy(piece, z, z).wait_recv()
        for z in others + [z_pos]:
            partner_copy(piece, z, z).wait_recv()
        part = piece_at(piece)
        mine, theirs = attended[part, :], attended_in[part, :]

        def term(step):
            cols = pl.ds(pl.multiple_of(lax.rem(y_pos + step, N_Y) * width, width), width)
            return (jnp.dot(mine, w_own[:, cols], preferred_element_type=jnp.float32)
                    + jnp.dot(theirs, w_other[:, cols], preferred_element_type=jnp.float32))

        way = lax.rem(piece, 2)
        relay_out[piece] = term(2).astype(jnp.bfloat16)
        relay_copy(piece).start()
        outbox[1 - way, piece] = term(3 - 2 * way).astype(jnp.bfloat16)
        direct_copy(1 - way, piece).start()
        pending[piece] = term(1 + 2 * way)
        kept[part, :] = term(0) + stream_ref[part, :].astype(jnp.float32)

    def combine(piece):
        relay_copy(piece).wait_recv()
        way = lax.rem(piece, 2)
        outbox[way, piece] = (pending[piece] + relay_in[piece].astype(jnp.float32)).astype(jnp.bfloat16)
        direct_copy(way, piece).start()

    @pl.when(high == 1)
    def _():
        def each(piece, carry):
            own_tile(piece)
            return carry

        lax.fori_loop(0, PIECES, each, 0)
        passes = []
        for index, (step, half) in enumerate(order):
            hops[index].wait_recv()
            landed = keyvals.at[0, source(step), :, core, halves[half]]
            copy = remote(landed, landed, t_send.at[index], t_recv.at[index], sibling)
            copy.start()
            passes.append(copy)
        for copy in passes:
            copy.wait()

    loads[1].wait()
    loads[2].wait()

    def stage(step, carry):
        @pl.when(step < PIECES)
        def _():
            @pl.when(high == 0)
            def _():
                own_tile(step)

            @pl.when(high == 1)
            def _():
                low_tile(step)

            complete(step)

        @pl.when(jnp.logical_and(step >= 1, step <= PIECES))
        def _():
            multiply(step - 1)

        @pl.when(step >= 2)
        def _():
            combine(step - 2)

        return carry

    lax.fori_loop(0, PIECES + 2, stage, 0)

    def finish(piece, carry):
        part = piece_at(piece)
        direct_copy(0, piece).wait_recv()
        direct_copy(1, piece).wait_recv()
        total = kept[part, :] + inbox[0, piece].astype(jnp.float32) + inbox[1, piece].astype(jnp.float32)
        out_ref[part, :] = total.astype(jnp.bfloat16)
        return carry

    lax.fori_loop(0, PIECES, finish, 0)

    def drain(piece, carry):
        for z in others:
            result_copy(piece, z, z_pos).wait_send()
        for z in others + [z_pos]:
            partner_copy(piece, z, z_pos).wait_send()
        relay_copy(piece).wait_send()
        direct_copy(0, piece).wait_send()
        direct_copy(1, piece).wait_send()
        return carry

    lax.fori_loop(0, PIECES, drain, 0)
    for copy in list(sent.values()) + list(z_copies.values()) + list(q_copies.values()) + shares:
        copy.wait_send()

    @pl.when(high == 0)
    def _():
        for hop in hops:
            hop.wait_send()


def attention(stream, gain_row, cosine, sine, weight, own_weight, other_half):
    rows, width = stream.shape
    head = HEAD
    dma = pltpu.SemaphoreType.DMA
    return pl.pallas_call(
        attention_kernel,
        out_shape=jax.ShapeDtypeStruct((rows, width), jnp.bfloat16),
        in_specs=whole(4) + [pl.BlockSpec(memory_space=pl.ANY)] * 3,
        out_specs=pl.BlockSpec(memory_space=pltpu.VMEM),
        scratch_shapes=[
            pltpu.VMEM((N_CH, rows, width), jnp.bfloat16),
            pltpu.VMEM(weight.shape, jnp.bfloat16),
            pltpu.VMEM((rows, weight.shape[1]), jnp.float32),
            pltpu.VMEM((rows, 128), jnp.float32),
            pltpu.VMEM((width // head, 3, rows, head), jnp.bfloat16),
            pltpu.VMEM((N_Z, rows, head), jnp.bfloat16),
            pltpu.VMEM((2, N_Z, 2, 2, rows, head), jnp.bfloat16),
            pltpu.VMEM((N_Z, rows, 2 * head), jnp.float32),
            pltpu.VMEM((N_Z, rows, head), jnp.float32),
            pltpu.VMEM((N_Z, rows, head), jnp.bfloat16),
            pltpu.VMEM((rows, width), jnp.bfloat16),
            pltpu.VMEM((rows, width), jnp.bfloat16),
            pltpu.VMEM((width, N_Y * width), jnp.bfloat16),
            pltpu.VMEM((width, N_Y * width), jnp.bfloat16),
        ] + box_shapes(rows, width) + [
            dma((3,)), dma((18,)), dma((18,)), dma((2, 2)), dma((2, 3)), dma((2, 3)), dma((2, 3)), dma((2, 3)),
            dma((8,)), dma((8,)), dma((8,)), dma((8,)), dma((8,)), dma((8,)),
            dma((PIECES, N_Z)), dma((PIECES, N_Z)), dma((PIECES, N_Z)), dma((PIECES, N_Z)),
        ],
        compiler_params=pltpu.CompilerParams(collective_id=3, has_side_effects=True, vmem_limit_bytes=VMEM_LIMIT),
        name="attention",
    )(stream, gain_row, cosine, sine, weight, own_weight, other_half)


def rotation_tables(rows):
    positions = lax.axis_index("ctx") * rows + jnp.arange(rows, dtype=jnp.int32)
    half_size = HEAD // 2
    frequency = 10000.0 ** (-jnp.arange(half_size, dtype=jnp.float32) * 2.0 / HEAD)
    angles = positions.astype(jnp.float32)[:, None] * frequency[None, :]
    cosine, sine = jnp.cos(angles), jnp.sin(angles)
    return jnp.concatenate([cosine, cosine], axis=1), jnp.concatenate([-sine, sine], axis=1)


def shards(features, residual_in, short_filter, medium_filter, skip_gain, out_weight, norm_gain, attn_weight,
           attn_out):
    rows = features.shape[0]
    cosine, sine = rotation_tables(rows)
    stream, attn_half = hyena(jnp.transpose(features, (1, 0, 2)), short_filter, medium_filter.T,
                              skip_gain[None, :], residual_in, out_weight, attn_out)
    return attention(stream, norm_gain[None, :], cosine, sine, attn_weight, attn_out, attn_half)


def solution(mesh):
    in_specs = (
        P("ctx", None, "ch"),
        P("ctx", "ch"),
        P(None, None, "ch"),
        P(None, "ch"),
        P("ch"),
        P("ch", None),
        P(),
        P(None, "ch"),
        P("ch", None),
    )
    out_specs = P("ctx", "ch")
    return jax.shard_map(shards, mesh=mesh, in_specs=in_specs, out_specs=out_specs, check_vma=False)
```

```python
import functools

import jax
import jax.numpy as jnp
from jax import lax
from jax.experimental import pallas as pl
from jax.experimental.pallas import tpu as pltpu
from jax.sharding import PartitionSpec as P

HEAD = 128
GROUP_SIZE = 16
N_CH = 8
N_CTX = 16
N_Y = 4
N_Z = 4
HALO = 144

norm_eps = 1e-05
MESH = pl.DeviceIdType.MESH
VMEM_LIMIT = 60 * 1024 * 1024


def remote(src, dst, send_sem, recv_sem, target):
    return pltpu.make_async_remote_copy(
        src_ref=src, dst_ref=dst, send_sem=send_sem, recv_sem=recv_sem,
        device_id=target, device_id_type=MESH,
    )


def greet(targets):
    barrier = pltpu.get_barrier_semaphore()
    for target in targets:
        pl.semaphore_signal(barrier, inc=1, device_id=target, device_id_type=MESH)
    pl.semaphore_wait(barrier, len(targets))


def whole(count):
    return [pl.BlockSpec(memory_space=pltpu.VMEM)] * count


def ring_z():
    ctx = lax.axis_index("ctx")
    chan = lax.axis_index("ch")
    core = lax.rem(ctx, 2)
    z_pos = lax.rem(ctx // 2, N_Z)
    base = ctx - z_pos * 2 - core
    sibling = (base + z_pos * 2 + 1 - core, chan)
    ring = [(base + lax.rem(z_pos + step, N_Z) * 2 + core, chan) for step in range(1, N_Z)]
    return core, z_pos, sibling, ring


def piece_rows(z_pos, core, tall):
    return pl.ds(pl.multiple_of((z_pos * 2 + core) * tall, tall), tall)


class Spread:
    def __init__(self, piece_ref, whole_ref, send_sem, recv_sem):
        self.piece, self.whole = piece_ref, whole_ref
        self.send, self.recv = send_sem, recv_sem
        self.core, self.z_pos, self.sibling, self.ring = ring_z()
        self.tall = whole_ref.shape[0] // (2 * N_Z)
        self.copies = []

    def push(self, src, rows, target):
        index = len(self.copies)
        copy = remote(src, self.whole.at[rows], self.send.at[index], self.recv.at[index], target)
        copy.start()
        self.copies.append(copy)

    def first(self):
        rows = piece_rows(self.z_pos, self.core, self.tall)
        for target in self.ring + [self.sibling]:
            self.push(self.piece, rows, target)

    def second(self):
        for step in (1, 3, 2):
            self.copies[step - 1].wait_recv()
            rows = piece_rows(lax.rem(self.z_pos + N_Z - step, N_Z), self.core, self.tall)
            self.push(self.whole.at[rows], rows, self.sibling)

    def finish(self):
        for copy in self.copies[3:]:
            copy.wait_recv()
        for copy in self.copies:
            copy.wait_send()


PIECES = 4


def column_places():
    ctx = lax.axis_index("ctx")
    chan = lax.axis_index("ch")
    y_pos = lax.rem(chan, N_Y)
    x_lo = chan // N_Y
    partner = (ctx, (1 - x_lo) * N_Y + y_pos)
    up = (ctx, x_lo * N_Y + lax.rem(y_pos + 1, N_Y))
    down = (ctx, x_lo * N_Y + lax.rem(y_pos + 3, N_Y))
    return y_pos, x_lo, partner, up, down


def piece_of(ref, piece):
    tall = ref.shape[0] // PIECES
    return ref.at[pl.ds(piece * tall, tall)]


def cross(left, left_in, partner, x_send, x_recv, piece):
    copy = remote(piece_of(left, piece), piece_of(left_in, piece), x_send.at[piece], x_recv.at[piece], partner)
    copy.start()
    return copy


def scatter_sum(left, left_in, crossing, base, out, w_own, w_other, boxes, up, down, y_pos):
    outbox, inbox, relay_out, relay_in, pending, kept, y_send, y_recv, r_send, r_recv = boxes
    rows, width = left.shape
    tall = rows // PIECES
    ways = (up, down)
    copies = []

    def term(piece, step):
        cols = pl.ds(pl.multiple_of(lax.rem(y_pos + step, N_Y) * width, width), width)
        part = pl.ds(piece * tall, tall)
        return (jnp.dot(left[part, :], w_own[:, cols], preferred_element_type=jnp.float32)
                + jnp.dot(left_in[part, :], w_other[:, cols], preferred_element_type=jnp.float32))

    def send(way, piece, value):
        outbox[way, piece] = value.astype(jnp.bfloat16)
        copy = remote(outbox.at[way, piece], inbox.at[way, piece], y_send.at[way, piece], y_recv.at[way, piece],
                      ways[way])
        copy.start()
        copies.append(copy)
        return copy

    arrivals = {}
    relays = []

    def combine(piece):
        relays[piece].wait_recv()
        way = piece % 2
        arrivals[way, piece] = send(way, piece, pending[piece] + relay_in[piece].astype(jnp.float32))

    for piece in range(PIECES):
        crossing[piece].wait_recv()
        way = piece % 2
        relay_out[piece] = term(piece, 2).astype(jnp.bfloat16)
        relay = remote(relay_out.at[piece], relay_in.at[piece], r_send.at[piece], r_recv.at[piece], ways[way])
        relay.start()
        relays.append(relay)
        arrivals[1 - way, piece] = send(1 - way, piece, term(piece, (1, 3)[1 - way]))
        pending[piece] = term(piece, (1, 3)[way])
        part = pl.ds(piece * tall, tall)
        kept[part, :] = term(piece, 0) + base[part, :].astype(jnp.float32)
        if piece:
            combine(piece - 1)
    combine(PIECES - 1)

    def finish():
        for piece in range(PIECES):
            part = pl.ds(piece * tall, tall)
            for way in (1 - piece % 2, piece % 2):
                arrivals[way, piece].wait_recv()
            total = kept[part, :] + inbox[0, piece].astype(jnp.float32) + inbox[1, piece].astype(jnp.float32)
            out[part, :] = total.astype(jnp.bfloat16)
        for copy in list(crossing) + copies + relays:
            copy.wait_send()

    return finish


def box_shapes(rows, width):
    tall = rows // PIECES
    dma = pltpu.SemaphoreType.DMA
    return [
        pltpu.VMEM((2, PIECES, tall, width), jnp.bfloat16),
        pltpu.VMEM((2, PIECES, tall, width), jnp.bfloat16),
        pltpu.VMEM((PIECES, tall, width), jnp.bfloat16),
        pltpu.VMEM((PIECES, tall, width), jnp.bfloat16),
        pltpu.VMEM((PIECES, tall, width), jnp.float32),
        pltpu.VMEM((rows, width), jnp.float32),
        dma((2, PIECES)), dma((2, PIECES)), dma((PIECES,)), dma((PIECES,)),
    ]


def hyena_kernel(feat_ref, short_ref, medium_ref, skip_ref, base_ref, first_weight, second_weight,
                 out_ref, second_half,
                 halo, ext, taps, product, product_t, query, mixed_t, send_sem, recv_sem,
                 w_own, first_half, gated, gated_in, w_sem, x_send, x_recv, g_send, g_recv,
                 w_send, w_recv, v_send, v_recv, *boxes):
    rows, chans = out_ref.shape
    ctx = lax.axis_index("ctx")
    chan = lax.axis_index("ch")
    after = (lax.rem(ctx + 1, N_CTX), chan)
    before = (lax.rem(ctx + N_CTX - 1, N_CTX), chan)
    y_pos, x_lo, partner, up, down = column_places()
    core, z_pos, sibling, ring = ring_z()
    span = first_half.shape[1]
    load_own = pltpu.make_async_copy(
        first_weight.at[:, pl.ds(pl.multiple_of(x_lo * span, span), span)], w_own, w_sem)
    load_own.start()
    greet([after, before, partner, sibling, up, down] + ring)
    near = remote(feat_ref.at[pl.ds(0, 1), pl.ds(rows - 16, 16)], halo.at[pl.ds(0, 1), pl.ds(HALO - 16, 16)],
                  send_sem.at[0], recv_sem.at[0], after)
    far = remote(feat_ref.at[pl.ds(1, 2), pl.ds(rows - HALO, HALO)], halo.at[pl.ds(1, 2)],
                 send_sem.at[1], recv_sem.at[1], after)
    near.start()
    far.start()
    tall = first_half.shape[0] // (2 * N_Z)
    mine = piece_rows(z_pos, core, tall)
    half = pl.ds(pl.multiple_of((1 - x_lo) * span, span), span)
    cross_first = remote(first_weight.at[mine, half], first_half.at[mine], x_send.at[0], x_recv.at[0], partner)
    cross_second = remote(second_weight.at[mine, half], second_half.at[mine], x_send.at[1], x_recv.at[1], partner)
    cross_first.start()
    spread = Spread(first_half.at[mine], first_half, w_send, w_recv)
    later = Spread(second_half.at[mine], second_half, v_send, v_recv)

    groups = short_ref.shape[2]
    widen = (lax.broadcasted_iota(jnp.int32, (groups, chans), 1) // GROUP_SIZE
              == lax.broadcasted_iota(jnp.int32, (groups, chans), 0)).astype(jnp.float32)
    for kind in range(3):
        taps[kind, 0:7, :] = jnp.dot(short_ref[kind], widen, preferred_element_type=jnp.float32,
                                     precision=lax.Precision.HIGHEST)
        ext[kind, HALO:, :] = feat_ref[kind].astype(jnp.float32)

    def featured(kind, first, count):
        slab = ext[kind, pl.ds(first - 8 if isinstance(first, int) else pl.multiple_of(first - 8, 8), count + 8), :]
        total = taps[kind, 0:1, :] * slab[8:]
        for tap in range(1, 7):
            total = total + taps[kind, tap : tap + 1, :] * pltpu.roll(slab, tap, 0)[8:]
        return total

    def main_rows(step, carry):
        first = pl.multiple_of(16 + step * 16, 16)
        query[pl.ds(first, 16), :] = featured(0, pl.multiple_of(first + HALO, 16), 16)
        product[pl.ds(first + 128, 16), :] = featured(1, pl.multiple_of(first + HALO, 16), 16) * featured(2, pl.multiple_of(first + HALO, 16), 16)
        return carry

    lax.fori_loop(0, 8, main_rows, 0)
    cross_first.wait_recv()
    spread.first()
    cross_second.start()
    lax.fori_loop(8, rows // 16 - 1, main_rows, 0)
    near.wait()
    far.wait()
    keep = (ctx > 0).astype(jnp.float32)
    ext[0, HALO - 16 : HALO, :] = halo[0, HALO - 16 : HALO, :].astype(jnp.float32) * keep
    for kind in (1, 2):
        ext[kind, 0:HALO, :] = halo[kind].astype(jnp.float32) * keep
    query[0:16, :] = featured(0, HALO, 16)

    def rim_rows(step, carry):
        first = pl.multiple_of(step * 16, 16)
        product[pl.ds(first, 16), :] = featured(1, pl.multiple_of(first + 16, 16), 16) * featured(2, pl.multiple_of(first + 16, 16), 16)
        return carry

    lax.fori_loop(0, 9, rim_rows, 0)
    for block in range(5):
        product_t[:, 128 * block : 128 * block + 128] = (
            product[128 * block : 128 * block + 128, :].T.astype(jnp.bfloat16))
    row = lax.broadcasted_iota(jnp.int32, (128, 128), 0)
    col = lax.broadcasted_iota(jnp.int32, (128, 128), 1)

    def one_group(group, carry):
        line = jnp.broadcast_to(medium_ref[pl.ds(group, 1), :], (128, 128))
        wheel = pltpu.roll(line, 0, 1, stride=1, stride_axis=0)
        table = jnp.concatenate([jnp.where(col < row, wheel, 0.0), jnp.where(col >= row, wheel, 0.0)],
                                axis=0).astype(jnp.bfloat16)
        lane = pl.ds(pl.multiple_of(group * GROUP_SIZE, GROUP_SIZE), GROUP_SIZE)
        window = jnp.concatenate(
            [product_t[lane, 128 * block : 128 * block + 256] for block in range(4)], axis=0)
        mix = jnp.dot(window, table, preferred_element_type=jnp.float32)
        for block in range(4):
            mixed_t[lane, 128 * block : 128 * block + 128] = mix[16 * block : 16 * block + 16, :]
        return carry

    lax.fori_loop(0, groups, one_group, 0)
    crossing = []
    for block in range(4):
        part = pl.ds(128 * block, 128)
        mix = mixed_t[:, part].T
        inner = product[pl.ds(128 * block + 128, 128), :].astype(jnp.bfloat16).astype(jnp.float32)
        gated[part, :] = (query[part, :] * (mix + skip_ref[...] * inner)).astype(jnp.bfloat16)
        crossing.append(cross(gated, gated_in, partner, g_send, g_recv, block))
    spread.second()
    cross_second.wait_recv()
    later.first()
    load_own.wait()
    spread.finish()
    finish = scatter_sum(gated, gated_in, crossing, base_ref, out_ref, w_own, first_half, boxes, up, down, y_pos)
    later.second()
    finish()
    cross_first.wait_send()
    cross_second.wait_send()
    later.finish()


def hyena(feats, short_filter, medium_t, skip_row, base, first_weight, second_weight):
    kinds, rows, chans = feats.shape
    deep, wide = first_weight.shape
    dma = pltpu.SemaphoreType.DMA
    anywhere = pl.BlockSpec(memory_space=pl.ANY)
    return pl.pallas_call(
        hyena_kernel,
        out_shape=(jax.ShapeDtypeStruct((rows, chans), jnp.bfloat16),
                   jax.ShapeDtypeStruct((deep, wide // 2), jnp.bfloat16)),
        in_specs=whole(5) + [anywhere] * 2,
        out_specs=(pl.BlockSpec(memory_space=pltpu.VMEM), anywhere),
        scratch_shapes=[
            pltpu.VMEM((3, HALO, chans), jnp.bfloat16),
            pltpu.VMEM((3, HALO + rows, chans), jnp.float32),
            pltpu.VMEM((3, 8, chans), jnp.float32),
            pltpu.VMEM((128 + rows, chans), jnp.float32),
            pltpu.VMEM((chans, 128 + rows), jnp.bfloat16),
            pltpu.VMEM((rows, chans), jnp.float32),
            pltpu.VMEM((chans, rows), jnp.float32),
            dma((2,)), dma((2,)),
            pltpu.VMEM((deep, wide // 2), jnp.bfloat16),
            pltpu.VMEM((deep, wide // 2), jnp.bfloat16),
            pltpu.VMEM((rows, chans), jnp.bfloat16),
            pltpu.VMEM((rows, chans), jnp.bfloat16),
            dma, dma((2,)), dma((2,)), dma((PIECES,)), dma((PIECES,)),
            dma((7,)), dma((7,)), dma((7,)), dma((7,)),
        ] + box_shapes(rows, chans),
        compiler_params=pltpu.CompilerParams(collective_id=0, has_side_effects=True, vmem_limit_bytes=VMEM_LIMIT),
        name="hyena",
    )(feats, short_filter, medium_t, skip_row, base, first_weight, second_weight)


def attention_kernel(stream_ref, gain_ref, cos_ref, sin_ref, weight_ref, own_ref, other_ref, out_ref,
                     blocks, w_ref, wide_acc, squares, qkv,
                     queries, keyvals, acc, peak, results, attended, attended_in, w_own, w_other,
                     outbox, inbox, relay_out, relay_in, pending, kept,
                     y_send, y_recv, r_send, r_recv,
                     w_sem, g_send, g_recv, own_sem, q_send, q_recv, z_send, z_recv, s_send, s_recv,
                     h_send, h_recv, t_send, t_recv, o_send, o_recv, p_send, p_recv, transit, d_send, d_recv):
    rows, width = stream_ref.shape
    head = HEAD
    heads = width // head
    tile = rows // PIECES
    tall = rows // 2
    ctx = lax.axis_index("ctx")
    core = lax.rem(ctx, 2)
    z_pos = lax.rem(ctx // 2, N_Z)
    high = ctx // (2 * N_Z)
    chan = lax.axis_index("ch")
    y_pos, x_lo, partner, dev_up, dev_down = column_places()
    up, down, opposite = lax.rem(y_pos + 1, N_Y), lax.rem(y_pos + 3, N_Y), lax.rem(y_pos + 2, N_Y)
    wide = w_own.shape[1]
    loads = [
        pltpu.make_async_copy(weight_ref, w_ref, w_sem.at[0]),
        pltpu.make_async_copy(own_ref.at[:, pl.ds(pl.multiple_of(x_lo * wide, wide), wide)], w_own, w_sem.at[1]),
        pltpu.make_async_copy(other_ref, w_other, w_sem.at[2]),
    ]
    for load in loads:
        load.start()

    def place(x, z, c):
        return ((x * N_Z + z) * 2 + c, chan)

    def partner_place(z):
        return ((high * N_Z + z) * 2 + core, (1 - x_lo) * N_Y + y_pos)

    sibling = place(high, z_pos, 1 - core)
    across = place(1 - high, z_pos, core)
    others = [lax.rem(z_pos + step, N_Z) for step in range(1, N_Z)]
    ring = [place(high, z, core) for z in others]
    diagonal = (((1 - high) * N_Z + z_pos) * 2 + core, (1 - x_lo) * N_Y + y_pos)
    greet([dev_up, dev_down, partner, sibling, across, diagonal] + ring + [partner_place(z) for z in others])

    def slot(x, y):
        return x * N_Y + y

    halves = [pl.ds(0, tall), pl.ds(tall, tall)]
    quarters = [[pl.ds(half * tall + number * (tall // 2), tall // 2) for number in range(2)] for half in range(2)]
    sent = {}

    def push(name, src, where, part, target):
        index = len(sent)
        copy = remote(src.at[part], blocks.at[where, part], g_send.at[index], g_recv.at[index], target)
        copy.start()
        sent[name] = copy

    mine, other = slot(x_lo, y_pos), slot(1 - x_lo, y_pos)
    above, below, far = slot(x_lo, up), slot(x_lo, down), slot(x_lo, opposite)

    def own_sends(half):
        part = halves[half]
        push(("x", half), stream_ref, mine, part, partner)
        push(("up", half), stream_ref, mine, part, dev_up)
        push(("down", half), stream_ref, mine, part, dev_down)

    def pass_on(half):
        first, second = quarters[half]
        part = halves[half]
        sent["up", half].wait_recv()
        push(("upup", half), blocks.at[below], below, first, dev_up)
        sent["down", half].wait_recv()
        push(("downdown", half), blocks.at[above], above, second, dev_down)
        sent["x", half].wait_recv()
        push(("xup", half), blocks.at[other], other, part, dev_up)
        push(("xdown", half), blocks.at[other], other, part, dev_down)

    def pass_far(half):
        first, second = quarters[half]
        sent["upup", half].wait_recv()
        push(("far0", half), blocks.at[far], far, first, partner)
        sent["downdown", half].wait_recv()
        push(("far1", half), blocks.at[far], far, second, partner)

    def use(src, where, half, fresh=False):
        part = halves[half]
        value = src[part, :].astype(jnp.float32)
        square = value * value
        partial = (square[:, 0:128] + square[:, 128:256]) + (square[:, 256:384] + square[:, 384:512])
        cols = pl.ds(pl.multiple_of(where * width, width), width)
        scaled = (value * gain_ref[:, cols]).astype(jnp.bfloat16)
        term = jnp.dot(scaled, w_ref[cols, :], preferred_element_type=jnp.float32)
        squares[part, :] = partial if fresh else squares[part, :] + partial
        wide_acc[part, :] = term if fresh else wide_acc[part, :] + term

    def last_uses(half):
        for names, y in ((("xdown",), up), (("xup",), down), (("far0", "far1"), opposite)):
            for name in names:
                sent[name, half].wait_recv()
            use(blocks.at[slot(1 - x_lo, y)], slot(1 - x_lo, y), half)

    scale = head ** -0.5 * 1.4426950408889634

    def heads_out(half):
        part = halves[half]
        inverse = lax.rsqrt(jnp.sum(squares[part, :], axis=1, keepdims=True) / (N_CH * width) + norm_eps)
        for number in range(heads):
            for kind in range(3):
                first = (number * 3 + kind) * head
                value = wide_acc[part, first : first + head] * inverse
                if kind < 2:
                    value = value * cos_ref[part, :] + pltpu.roll(value, head // 2, 1) * sin_ref[part, :]
                if kind == 0:
                    value = value * scale
                qkv[number, kind, part, :] = value.astype(jnp.bfloat16)

    z_copies, q_copies, own_copies = {}, {}, []

    def exchange(half):
        part = halves[half]
        own_kv = pltpu.make_async_copy(qkv.at[z_pos, pl.ds(1, 2), part],
                                       keyvals.at[high, z_pos, :, core, part], own_sem.at[half, 1])
        own_q = pltpu.make_async_copy(qkv.at[z_pos, 0, part], queries.at[z_pos, part], own_sem.at[half, 0])
        own_kv.start()
        own_q.start()
        own_copies.append((own_kv, own_q))
        for step in (1, 2, 3):
            copy = remote(qkv.at[others[step - 1], pl.ds(1, 2), part], keyvals.at[high, z_pos, :, core, part],
                          z_send.at[half, step - 1], z_recv.at[half, step - 1], ring[step - 1])
            copy.start()
            z_copies[half, step] = copy
        for step in (1, 2, 3):
            copy = remote(qkv.at[others[step - 1], 0, part], queries.at[z_pos, part],
                          q_send.at[half, step - 1], q_recv.at[half, step - 1], ring[step - 1])
            copy.start()
            q_copies[half, step] = copy

    own_sends(0)
    loads[0].wait()
    use(stream_ref, mine, 0, True)
    pass_on(0)
    own_sends(1)
    use(blocks.at[above], above, 0)
    use(blocks.at[below], below, 0)
    use(blocks.at[other], other, 0)
    pass_far(0)
    use(blocks.at[far], far, 0)
    use(stream_ref, mine, 1, True)
    last_uses(0)
    heads_out(0)
    exchange(0)
    pass_on(1)
    use(blocks.at[above], above, 1)
    use(blocks.at[below], below, 1)
    pass_far(1)
    use(blocks.at[other], other, 1)
    use(blocks.at[far], far, 1)
    last_uses(1)
    heads_out(1)
    exchange(1)

    def source(step):
        return lax.rem(z_pos + N_Z - step, N_Z)

    shares, hops = [], []

    def spread(step, half):
        index = len(shares)
        place_here = keyvals.at[high, source(step), :, core, halves[half]]
        share = remote(place_here, place_here, s_send.at[index], s_recv.at[index], sibling)
        share.start()
        shares.append(share)
        if half == 0:
            hop = remote(place_here, place_here, h_send.at[index], h_recv.at[index], across)
        else:
            hop = remote(place_here, transit.at[step], h_send.at[index], h_recv.at[index], diagonal)
        hops.append(hop)

        @pl.when(high == 0)
        def _():
            hop.start()

    order = [(step, half) for half in range(2) for step in (0, 1, 3, 2)]
    for step, half in order:
        if step:
            z_copies[half, step].wait_recv()
        else:
            own_copies[half][0].wait()
        spread(step, half)
    for pair in own_copies:
        pair[1].wait()
    for copy in list(q_copies.values()) + shares:
        copy.wait_recv()

    span = 2 * rows
    row = lax.broadcasted_iota(jnp.int32, (tile, span), 0) + core * rows
    col = lax.broadcasted_iota(jnp.int32, (tile, span), 1)
    ones = jnp.ones((span, head), jnp.bfloat16)

    def piece_at(piece):
        return pl.ds(pl.multiple_of(piece * tile, tile), tile)

    def update(block, part, first, z, diagonal):
        fold(block, part, first, keyvals[high, z, 0].reshape(span, head), keyvals[high, z, 1].reshape(span, head), diagonal)

    def fold(block, part, first, keys, plain_values, diagonal):
        values = jnp.concatenate([plain_values, ones], axis=1)
        scores = lax.dot_general(queries[block, part], keys, (((1,), (1,)), ((), ())),
                                 preferred_element_type=jnp.float32)
        if diagonal:
            scores = jnp.where(col <= row + first, scores, -1e30)
        top = jnp.max(scores, axis=1, keepdims=True)
        if diagonal:
            new = jnp.broadcast_to(top, (tile, head))
        else:
            old = peak[block, part]
            new = jnp.maximum(old, top)
            shrink = jnp.exp2(old - new)
        peak[block, part] = new
        weights = jnp.exp2(scores - jnp.concatenate([new] * (span // head), axis=1)).astype(jnp.bfloat16)
        term = jnp.dot(weights, values, preferred_element_type=jnp.float32)
        if not diagonal:
            term = acc[block, part] * jnp.concatenate([shrink, shrink], axis=1) + term
        acc[block, part] = term

    def own_tile(piece):
        part, first = piece_at(piece), piece * tile
        for block in range(N_Z):
            update(block, part, first, block, True)
        for z in range(N_Z - 1):
            for block in range(z + 1, N_Z):
                update(block, part, first, z, False)

    def low_tile(piece, half):
        part, first = piece_at(piece), piece * tile

        def each(pair, carry):
            keys, values = [
                jnp.concatenate([keyvals[0, 2 * pair + number, kind, side, halves[half], :]
                                 for number in range(2) for side in range(2)], axis=0)
                for kind in range(2)
            ]
            for block in range(N_Z):
                fold(block, part, first, keys, values, False)
            return carry

        lax.fori_loop(0, N_Z // 2, each, 0)

    lanes = pl.ds(pl.multiple_of(z_pos * head, head), head)

    def result_copy(piece, block, owner):
        columns = pl.ds(pl.multiple_of(owner * head, head), head)
        part = piece_at(piece)
        return remote(results.at[block, part], attended.at[part, columns], o_send.at[piece, block],
                      o_recv.at[piece, owner], place(high, block, core))

    def partner_copy(piece, block, owner):
        columns = pl.ds(pl.multiple_of(owner * head, head), head)
        part = piece_at(piece)
        return remote(results.at[block, part], attended_in.at[part, columns], p_send.at[piece, block],
                      p_recv.at[piece, owner], partner_place(block))

    def complete(piece):
        part = piece_at(piece)

        def each(block, carry):
            total = acc[block, part]
            results[block, part] = (total[:, :head] / total[:, head:]).astype(jnp.bfloat16)
            partner_copy(piece, block, z_pos).start()

            @pl.when(block != z_pos)
            def _():
                result_copy(piece, block, z_pos).start()

            @pl.when(block == z_pos)
            def _():
                attended[part, lanes] = results[block, part]

            return carry

        lax.fori_loop(0, N_Z, each, 0)

    def way_place(way):
        return (ctx, x_lo * N_Y + lax.rem(y_pos + 1 + 2 * way, N_Y))

    def relay_copy(piece):
        return remote(relay_out.at[piece], relay_in.at[piece], r_send.at[piece], r_recv.at[piece],
                      way_place(lax.rem(piece, 2)))

    def direct_copy(way, piece):
        return remote(outbox.at[way, piece], inbox.at[way, piece], y_send.at[way, piece], y_recv.at[way, piece],
                      way_place(way))

    def multiply(piece):
        for z in others:
            result_copy(piece, z, z).wait_recv()
        for z in others + [z_pos]:
            partner_copy(piece, z, z).wait_recv()
        part = piece_at(piece)
        mine, theirs = attended[part, :], attended_in[part, :]

        def term(step):
            cols = pl.ds(pl.multiple_of(lax.rem(y_pos + step, N_Y) * width, width), width)
            return (jnp.dot(mine, w_own[:, cols], preferred_element_type=jnp.float32)
                    + jnp.dot(theirs, w_other[:, cols], preferred_element_type=jnp.float32))

        way = lax.rem(piece, 2)
        relay_out[piece] = term(2).astype(jnp.bfloat16)
        relay_copy(piece).start()
        outbox[1 - way, piece] = term(3 - 2 * way).astype(jnp.bfloat16)
        direct_copy(1 - way, piece).start()
        pending[piece] = term(1 + 2 * way)
        kept[part, :] = term(0) + stream_ref[part, :].astype(jnp.float32)

    def combine(piece):
        relay_copy(piece).wait_recv()
        way = lax.rem(piece, 2)
        outbox[way, piece] = (pending[piece] + relay_in[piece].astype(jnp.float32)).astype(jnp.bfloat16)
        direct_copy(way, piece).start()

    @pl.when(high == 1)
    def _():
        passes, legs = [], []

        def landed(index):
            step, half = order[index]
            return keyvals.at[0, source(step), :, core, halves[half]]

        def forward(index):
            copy = remote(landed(index), landed(index), t_send.at[index], t_recv.at[index], sibling)
            copy.start()
            passes.append(copy)

        for index in range(4):
            hops[index].wait_recv()
            forward(index)
        for index in range(4, 8):
            own_tile(index - 4)
            hops[index].wait_recv()
            leg = remote(transit.at[order[index][0]], landed(index), d_send.at[index - 4], d_recv.at[index - 4], partner)
            leg.start()
            legs.append(leg)
        for copy in passes:
            copy.wait_recv()

        def each(piece, carry):
            low_tile(piece, 0)
            return carry

        lax.fori_loop(0, PIECES // 2, each, 0)
        for index in range(4, 8):
            legs[index - 4].wait_recv()
            forward(index)
        lax.fori_loop(PIECES // 2, PIECES, each, 0)
        for copy in passes[4:]:
            copy.wait_recv()
        for copy in passes:
            copy.wait_send()
        for leg in legs:
            leg.wait_send()

    loads[1].wait()
    loads[2].wait()

    def stage(step, carry):
        @pl.when(step < PIECES)
        def _():
            @pl.when(high == 0)
            def _():
                own_tile(step)

            @pl.when(high == 1)
            def _():
                low_tile(step, 1)

            complete(step)

        @pl.when(jnp.logical_and(step >= 1, step <= PIECES))
        def _():
            multiply(step - 1)

        @pl.when(step >= 2)
        def _():
            combine(step - 2)

        return carry

    lax.fori_loop(0, PIECES + 2, stage, 0)

    def finish(piece, carry):
        part = piece_at(piece)
        direct_copy(0, piece).wait_recv()
        direct_copy(1, piece).wait_recv()
        total = kept[part, :] + inbox[0, piece].astype(jnp.float32) + inbox[1, piece].astype(jnp.float32)
        out_ref[part, :] = total.astype(jnp.bfloat16)
        return carry

    lax.fori_loop(0, PIECES, finish, 0)

    def drain(piece, carry):
        for z in others:
            result_copy(piece, z, z_pos).wait_send()
        for z in others + [z_pos]:
            partner_copy(piece, z, z_pos).wait_send()
        relay_copy(piece).wait_send()
        direct_copy(0, piece).wait_send()
        direct_copy(1, piece).wait_send()
        return carry

    lax.fori_loop(0, PIECES, drain, 0)
    for copy in list(sent.values()) + list(z_copies.values()) + list(q_copies.values()) + shares:
        copy.wait_send()

    @pl.when(high == 0)
    def _():
        for hop in hops:
            hop.wait_send()


def attention(stream, gain_row, cosine, sine, weight, own_weight, other_half):
    rows, width = stream.shape
    head = HEAD
    dma = pltpu.SemaphoreType.DMA
    return pl.pallas_call(
        attention_kernel,
        out_shape=jax.ShapeDtypeStruct((rows, width), jnp.bfloat16),
        in_specs=whole(4) + [pl.BlockSpec(memory_space=pl.ANY)] * 3,
        out_specs=pl.BlockSpec(memory_space=pltpu.VMEM),
        scratch_shapes=[
            pltpu.VMEM((N_CH, rows, width), jnp.bfloat16),
            pltpu.VMEM(weight.shape, jnp.bfloat16),
            pltpu.VMEM((rows, weight.shape[1]), jnp.float32),
            pltpu.VMEM((rows, 128), jnp.float32),
            pltpu.VMEM((width // head, 3, rows, head), jnp.bfloat16),
            pltpu.VMEM((N_Z, rows, head), jnp.bfloat16),
            pltpu.VMEM((2, N_Z, 2, 2, rows, head), jnp.bfloat16),
            pltpu.VMEM((N_Z, rows, 2 * head), jnp.float32),
            pltpu.VMEM((N_Z, rows, head), jnp.float32),
            pltpu.VMEM((N_Z, rows, head), jnp.bfloat16),
            pltpu.VMEM((rows, width), jnp.bfloat16),
            pltpu.VMEM((rows, width), jnp.bfloat16),
            pltpu.VMEM((width, N_Y * width), jnp.bfloat16),
            pltpu.VMEM((width, N_Y * width), jnp.bfloat16),
        ] + box_shapes(rows, width) + [
            dma((3,)), dma((18,)), dma((18,)), dma((2, 2)), dma((2, 3)), dma((2, 3)), dma((2, 3)), dma((2, 3)),
            dma((8,)), dma((8,)), dma((8,)), dma((8,)), dma((8,)), dma((8,)),
            dma((PIECES, N_Z)), dma((PIECES, N_Z)), dma((PIECES, N_Z)), dma((PIECES, N_Z)),
            pltpu.VMEM((N_Z, 2, rows // 2, head), jnp.bfloat16), dma((4,)), dma((4,)),
        ],
        compiler_params=pltpu.CompilerParams(collective_id=3, has_side_effects=True, vmem_limit_bytes=VMEM_LIMIT),
        name="attention",
    )(stream, gain_row, cosine, sine, weight, own_weight, other_half)


def rotation_tables(rows):
    positions = lax.axis_index("ctx") * rows + jnp.arange(rows, dtype=jnp.int32)
    half_size = HEAD // 2
    frequency = 10000.0 ** (-jnp.arange(half_size, dtype=jnp.float32) * 2.0 / HEAD)
    angles = positions.astype(jnp.float32)[:, None] * frequency[None, :]
    cosine, sine = jnp.cos(angles), jnp.sin(angles)
    return jnp.concatenate([cosine, cosine], axis=1), jnp.concatenate([-sine, sine], axis=1)


def shards(features, residual_in, short_filter, medium_filter, skip_gain, out_weight, norm_gain, attn_weight,
           attn_out):
    rows = features.shape[0]
    cosine, sine = rotation_tables(rows)
    stream, attn_half = hyena(jnp.transpose(features, (1, 0, 2)), short_filter, medium_filter.T,
                              skip_gain[None, :], residual_in, out_weight, attn_out)
    return attention(stream, norm_gain[None, :], cosine, sine, attn_weight, attn_out, attn_half)


def solution(mesh):
    in_specs = (
        P("ctx", None, "ch"),
        P("ctx", "ch"),
        P(None, None, "ch"),
        P(None, "ch"),
        P("ch"),
        P("ch", None),
        P(),
        P(None, "ch"),
        P("ch", None),
    )
    out_specs = P("ctx", "ch")
    return jax.shard_map(shards, mesh=mesh, in_specs=in_specs, out_specs=out_specs, check_vma=False)
```

```python
import functools

import jax
import jax.numpy as jnp
from jax import lax
from jax.experimental import pallas as pl
from jax.experimental.pallas import tpu as pltpu
from jax.sharding import PartitionSpec as P

HEAD = 128
GROUP_SIZE = 16
N_CH = 8
N_CTX = 16
N_Y = 4
N_Z = 4
HALO = 144

norm_eps = 1e-05
MESH = pl.DeviceIdType.MESH
VMEM_LIMIT = 60 * 1024 * 1024


def remote(src, dst, send_sem, recv_sem, target):
    return pltpu.make_async_remote_copy(
        src_ref=src, dst_ref=dst, send_sem=send_sem, recv_sem=recv_sem,
        device_id=target, device_id_type=MESH,
    )


def greet(targets):
    barrier = pltpu.get_barrier_semaphore()
    for target in targets:
        pl.semaphore_signal(barrier, inc=1, device_id=target, device_id_type=MESH)
    pl.semaphore_wait(barrier, len(targets))


def whole(count):
    return [pl.BlockSpec(memory_space=pltpu.VMEM)] * count


def ring_z():
    ctx = lax.axis_index("ctx")
    chan = lax.axis_index("ch")
    core = lax.rem(ctx, 2)
    z_pos = lax.rem(ctx // 2, N_Z)
    base = ctx - z_pos * 2 - core
    sibling = (base + z_pos * 2 + 1 - core, chan)
    ring = [(base + lax.rem(z_pos + step, N_Z) * 2 + core, chan) for step in range(1, N_Z)]
    return core, z_pos, sibling, ring


def piece_rows(z_pos, core, tall):
    return pl.ds(pl.multiple_of((z_pos * 2 + core) * tall, tall), tall)


class Spread:
    def __init__(self, piece_ref, whole_ref, send_sem, recv_sem):
        self.piece, self.whole = piece_ref, whole_ref
        self.send, self.recv = send_sem, recv_sem
        self.core, self.z_pos, self.sibling, self.ring = ring_z()
        self.tall = whole_ref.shape[0] // (2 * N_Z)
        self.copies = []

    def push(self, src, rows, target):
        index = len(self.copies)
        copy = remote(src, self.whole.at[rows], self.send.at[index], self.recv.at[index], target)
        copy.start()
        self.copies.append(copy)

    def first(self):
        rows = piece_rows(self.z_pos, self.core, self.tall)
        for target in self.ring + [self.sibling]:
            self.push(self.piece, rows, target)

    def second(self):
        for step in (1, 3, 2):
            self.copies[step - 1].wait_recv()
            rows = piece_rows(lax.rem(self.z_pos + N_Z - step, N_Z), self.core, self.tall)
            self.push(self.whole.at[rows], rows, self.sibling)

    def finish(self):
        for copy in self.copies[3:]:
            copy.wait_recv()
        for copy in self.copies:
            copy.wait_send()


PIECES = 4


def column_places():
    ctx = lax.axis_index("ctx")
    chan = lax.axis_index("ch")
    y_pos = lax.rem(chan, N_Y)
    x_lo = chan // N_Y
    partner = (ctx, (1 - x_lo) * N_Y + y_pos)
    up = (ctx, x_lo * N_Y + lax.rem(y_pos + 1, N_Y))
    down = (ctx, x_lo * N_Y + lax.rem(y_pos + 3, N_Y))
    return y_pos, x_lo, partner, up, down


def piece_of(ref, piece):
    tall = ref.shape[0] // PIECES
    return ref.at[pl.ds(piece * tall, tall)]


def cross(left, left_in, partner, x_send, x_recv, piece):
    copy = remote(piece_of(left, piece), piece_of(left_in, piece), x_send.at[piece], x_recv.at[piece], partner)
    copy.start()
    return copy


def scatter_sum(left, left_in, crossing, base, out, w_own, w_other, boxes, up, down, y_pos):
    outbox, inbox, relay_out, relay_in, pending, kept, y_send, y_recv, r_send, r_recv = boxes
    rows, width = left.shape
    tall = rows // PIECES
    ways = (up, down)
    copies = []

    def term(piece, step):
        cols = pl.ds(pl.multiple_of(lax.rem(y_pos + step, N_Y) * width, width), width)
        part = pl.ds(piece * tall, tall)
        return (jnp.dot(left[part, :], w_own[:, cols], preferred_element_type=jnp.float32)
                + jnp.dot(left_in[part, :], w_other[:, cols], preferred_element_type=jnp.float32))

    def send(way, piece, value):
        outbox[way, piece] = value.astype(jnp.bfloat16)
        copy = remote(outbox.at[way, piece], inbox.at[way, piece], y_send.at[way, piece], y_recv.at[way, piece],
                      ways[way])
        copy.start()
        copies.append(copy)
        return copy

    arrivals = {}
    relays = []

    def combine(piece):
        relays[piece].wait_recv()
        way = piece % 2
        arrivals[way, piece] = send(way, piece, pending[piece] + relay_in[piece].astype(jnp.float32))

    for piece in range(PIECES):
        crossing[piece].wait_recv()
        way = piece % 2
        relay_out[piece] = term(piece, 2).astype(jnp.bfloat16)
        relay = remote(relay_out.at[piece], relay_in.at[piece], r_send.at[piece], r_recv.at[piece], ways[way])
        relay.start()
        relays.append(relay)
        arrivals[1 - way, piece] = send(1 - way, piece, term(piece, (1, 3)[1 - way]))
        pending[piece] = term(piece, (1, 3)[way])
        part = pl.ds(piece * tall, tall)
        kept[part, :] = term(piece, 0) + base[part, :].astype(jnp.float32)
        if piece:
            combine(piece - 1)
    combine(PIECES - 1)

    def finish():
        for piece in range(PIECES):
            part = pl.ds(piece * tall, tall)
            for way in (1 - piece % 2, piece % 2):
                arrivals[way, piece].wait_recv()
            total = kept[part, :] + inbox[0, piece].astype(jnp.float32) + inbox[1, piece].astype(jnp.float32)
            out[part, :] = total.astype(jnp.bfloat16)
        for copy in list(crossing) + copies + relays:
            copy.wait_send()

    return finish


def box_shapes(rows, width):
    tall = rows // PIECES
    dma = pltpu.SemaphoreType.DMA
    return [
        pltpu.VMEM((2, PIECES, tall, width), jnp.bfloat16),
        pltpu.VMEM((2, PIECES, tall, width), jnp.bfloat16),
        pltpu.VMEM((PIECES, tall, width), jnp.bfloat16),
        pltpu.VMEM((PIECES, tall, width), jnp.bfloat16),
        pltpu.VMEM((PIECES, tall, width), jnp.float32),
        pltpu.VMEM((rows, width), jnp.float32),
        dma((2, PIECES)), dma((2, PIECES)), dma((PIECES,)), dma((PIECES,)),
    ]


def hyena_kernel(feat_ref, short_ref, medium_ref, skip_ref, base_ref, first_weight, second_weight,
                 out_ref, second_half,
                 halo, ext, taps, product, product_t, query, mixed_t, send_sem, recv_sem,
                 w_own, first_half, gated, gated_in, w_sem, x_send, x_recv, g_send, g_recv,
                 w_send, w_recv, v_send, v_recv, *boxes):
    rows, chans = out_ref.shape
    ctx = lax.axis_index("ctx")
    chan = lax.axis_index("ch")
    after = (lax.rem(ctx + 1, N_CTX), chan)
    before = (lax.rem(ctx + N_CTX - 1, N_CTX), chan)
    y_pos, x_lo, partner, up, down = column_places()
    core, z_pos, sibling, ring = ring_z()
    span = first_half.shape[1]
    load_own = pltpu.make_async_copy(
        first_weight.at[:, pl.ds(pl.multiple_of(x_lo * span, span), span)], w_own, w_sem)
    load_own.start()
    greet([after, before, partner, sibling, up, down] + ring)
    near = remote(feat_ref.at[pl.ds(0, 1), pl.ds(rows - 16, 16)], halo.at[pl.ds(0, 1), pl.ds(HALO - 16, 16)],
                  send_sem.at[0], recv_sem.at[0], after)
    far = remote(feat_ref.at[pl.ds(1, 2), pl.ds(rows - HALO, HALO)], halo.at[pl.ds(1, 2)],
                 send_sem.at[1], recv_sem.at[1], after)
    near.start()
    far.start()
    tall = first_half.shape[0] // (2 * N_Z)
    mine = piece_rows(z_pos, core, tall)
    half = pl.ds(pl.multiple_of((1 - x_lo) * span, span), span)
    cross_first = remote(first_weight.at[mine, half], first_half.at[mine], x_send.at[0], x_recv.at[0], partner)
    cross_second = remote(second_weight.at[mine, half], second_half.at[mine], x_send.at[1], x_recv.at[1], partner)
    cross_first.start()
    spread = Spread(first_half.at[mine], first_half, w_send, w_recv)
    later = Spread(second_half.at[mine], second_half, v_send, v_recv)

    groups = short_ref.shape[2]
    widen = (lax.broadcasted_iota(jnp.int32, (groups, chans), 1) // GROUP_SIZE
              == lax.broadcasted_iota(jnp.int32, (groups, chans), 0)).astype(jnp.float32)
    for kind in range(3):
        taps[kind, 0:7, :] = jnp.dot(short_ref[kind], widen, preferred_element_type=jnp.float32,
                                     precision=lax.Precision.HIGHEST)
        ext[kind, HALO:, :] = feat_ref[kind].astype(jnp.float32)

    def featured(kind, first, count):
        slab = ext[kind, pl.ds(first - 8 if isinstance(first, int) else pl.multiple_of(first - 8, 8), count + 8), :]
        total = taps[kind, 0:1, :] * slab[8:]
        for tap in range(1, 7):
            total = total + taps[kind, tap : tap + 1, :] * pltpu.roll(slab, tap, 0)[8:]
        return total

    def main_rows(step, carry):
        first = pl.multiple_of(16 + step * 16, 16)
        query[pl.ds(first, 16), :] = featured(0, pl.multiple_of(first + HALO, 16), 16)
        product[pl.ds(first + 128, 16), :] = featured(1, pl.multiple_of(first + HALO, 16), 16) * featured(2, pl.multiple_of(first + HALO, 16), 16)
        return carry

    lax.fori_loop(0, 8, main_rows, 0)
    cross_first.wait_recv()
    spread.first()
    cross_second.start()
    lax.fori_loop(8, rows // 16 - 1, main_rows, 0)
    near.wait()
    far.wait()
    keep = (ctx > 0).astype(jnp.float32)
    ext[0, HALO - 16 : HALO, :] = halo[0, HALO - 16 : HALO, :].astype(jnp.float32) * keep
    for kind in (1, 2):
        ext[kind, 0:HALO, :] = halo[kind].astype(jnp.float32) * keep
    query[0:16, :] = featured(0, HALO, 16)

    def rim_rows(step, carry):
        first = pl.multiple_of(step * 16, 16)
        product[pl.ds(first, 16), :] = featured(1, pl.multiple_of(first + 16, 16), 16) * featured(2, pl.multiple_of(first + 16, 16), 16)
        return carry

    lax.fori_loop(0, 9, rim_rows, 0)
    for block in range(5):
        product_t[:, 128 * block : 128 * block + 128] = (
            product[128 * block : 128 * block + 128, :].T.astype(jnp.bfloat16))
    row = lax.broadcasted_iota(jnp.int32, (128, 128), 0)
    col = lax.broadcasted_iota(jnp.int32, (128, 128), 1)

    def one_group(group, carry):
        line = jnp.broadcast_to(medium_ref[pl.ds(group, 1), :], (128, 128))
        wheel = pltpu.roll(line, 0, 1, stride=1, stride_axis=0)
        table = jnp.concatenate([jnp.where(col < row, wheel, 0.0), jnp.where(col >= row, wheel, 0.0)],
                                axis=0).astype(jnp.bfloat16)
        lane = pl.ds(pl.multiple_of(group * GROUP_SIZE, GROUP_SIZE), GROUP_SIZE)
        window = jnp.concatenate(
            [product_t[lane, 128 * block : 128 * block + 256] for block in range(4)], axis=0)
        mix = jnp.dot(window, table, preferred_element_type=jnp.float32)
        for block in range(4):
            mixed_t[lane, 128 * block : 128 * block + 128] = mix[16 * block : 16 * block + 16, :]
        return carry

    lax.fori_loop(0, groups, one_group, 0)
    crossing = []
    for block in range(4):
        part = pl.ds(128 * block, 128)
        mix = mixed_t[:, part].T
        inner = product[pl.ds(128 * block + 128, 128), :].astype(jnp.bfloat16).astype(jnp.float32)
        gated[part, :] = (query[part, :] * (mix + skip_ref[...] * inner)).astype(jnp.bfloat16)
        crossing.append(cross(gated, gated_in, partner, g_send, g_recv, block))
    spread.second()
    cross_second.wait_recv()
    later.first()
    load_own.wait()
    spread.finish()
    finish = scatter_sum(gated, gated_in, crossing, base_ref, out_ref, w_own, first_half, boxes, up, down, y_pos)
    later.second()
    finish()
    cross_first.wait_send()
    cross_second.wait_send()
    later.finish()


def hyena(feats, short_filter, medium_t, skip_row, base, first_weight, second_weight):
    kinds, rows, chans = feats.shape
    deep, wide = first_weight.shape
    dma = pltpu.SemaphoreType.DMA
    anywhere = pl.BlockSpec(memory_space=pl.ANY)
    return pl.pallas_call(
        hyena_kernel,
        out_shape=(jax.ShapeDtypeStruct((rows, chans), jnp.bfloat16),
                   jax.ShapeDtypeStruct((deep, wide // 2), jnp.bfloat16)),
        in_specs=whole(5) + [anywhere] * 2,
        out_specs=(pl.BlockSpec(memory_space=pltpu.VMEM), anywhere),
        scratch_shapes=[
            pltpu.VMEM((3, HALO, chans), jnp.bfloat16),
            pltpu.VMEM((3, HALO + rows, chans), jnp.float32),
            pltpu.VMEM((3, 8, chans), jnp.float32),
            pltpu.VMEM((128 + rows, chans), jnp.float32),
            pltpu.VMEM((chans, 128 + rows), jnp.bfloat16),
            pltpu.VMEM((rows, chans), jnp.float32),
            pltpu.VMEM((chans, rows), jnp.float32),
            dma((2,)), dma((2,)),
            pltpu.VMEM((deep, wide // 2), jnp.bfloat16),
            pltpu.VMEM((deep, wide // 2), jnp.bfloat16),
            pltpu.VMEM((rows, chans), jnp.bfloat16),
            pltpu.VMEM((rows, chans), jnp.bfloat16),
            dma, dma((2,)), dma((2,)), dma((PIECES,)), dma((PIECES,)),
            dma((7,)), dma((7,)), dma((7,)), dma((7,)),
        ] + box_shapes(rows, chans),
        compiler_params=pltpu.CompilerParams(collective_id=0, has_side_effects=True, vmem_limit_bytes=VMEM_LIMIT),
        name="hyena",
    )(feats, short_filter, medium_t, skip_row, base, first_weight, second_weight)


def attention_kernel(stream_ref, gain_ref, cos_ref, sin_ref, weight_ref, own_ref, other_ref, out_ref,
                     blocks, w_ref, wide_acc, squares, qkv,
                     queries, keyvals, acc, peak, results, attended, attended_in, w_own, w_other,
                     outbox, inbox, relay_out, relay_in, pending, kept,
                     y_send, y_recv, r_send, r_recv,
                     w_sem, g_send, g_recv, own_sem, q_send, q_recv, z_send, z_recv, s_send, s_recv,
                     h_send, h_recv, t_send, t_recv, o_send, o_recv, p_send, p_recv, transit, d_send, d_recv):
    rows, width = stream_ref.shape
    head = HEAD
    heads = width // head
    tile = rows // PIECES
    tall = rows // 2
    ctx = lax.axis_index("ctx")
    core = lax.rem(ctx, 2)
    z_pos = lax.rem(ctx // 2, N_Z)
    high = ctx // (2 * N_Z)
    chan = lax.axis_index("ch")
    y_pos, x_lo, partner, dev_up, dev_down = column_places()
    up, down, opposite = lax.rem(y_pos + 1, N_Y), lax.rem(y_pos + 3, N_Y), lax.rem(y_pos + 2, N_Y)
    wide = w_own.shape[1]
    loads = [
        pltpu.make_async_copy(weight_ref, w_ref, w_sem.at[0]),
        pltpu.make_async_copy(own_ref.at[:, pl.ds(pl.multiple_of(x_lo * wide, wide), wide)], w_own, w_sem.at[1]),
        pltpu.make_async_copy(other_ref, w_other, w_sem.at[2]),
    ]
    for load in loads:
        load.start()

    def place(x, z, c):
        return ((x * N_Z + z) * 2 + c, chan)

    def partner_place(z):
        return ((high * N_Z + z) * 2 + core, (1 - x_lo) * N_Y + y_pos)

    sibling = place(high, z_pos, 1 - core)
    across = place(1 - high, z_pos, core)
    others = [lax.rem(z_pos + step, N_Z) for step in range(1, N_Z)]
    ring = [place(high, z, core) for z in others]
    diagonal = (((1 - high) * N_Z + z_pos) * 2 + core, (1 - x_lo) * N_Y + y_pos)
    greet([dev_up, dev_down, (ctx, x_lo * N_Y + opposite), partner, sibling, across, diagonal] + ring + [partner_place(z) for z in others])

    def slot(x, y):
        return x * N_Y + y

    halves = [pl.ds(0, tall), pl.ds(tall, tall)]
    quarters = [[pl.ds(half * tall + number * (tall // 2), tall // 2) for number in range(2)] for half in range(2)]
    sent = {}

    def push(name, src, where, part, target):
        index = len(sent)
        copy = remote(src.at[part], blocks.at[where, part], g_send.at[index], g_recv.at[index], target)
        copy.start()
        sent[name] = copy

    mine, other = slot(x_lo, y_pos), slot(1 - x_lo, y_pos)
    above, below, far = slot(x_lo, up), slot(x_lo, down), slot(x_lo, opposite)

    def own_sends(half):
        part = halves[half]
        push(("x", half), stream_ref, mine, part, partner)
        push(("up", half), stream_ref, mine, part, dev_up)
        push(("down", half), stream_ref, mine, part, dev_down)

    def pass_on(half):
        first, second = quarters[half]
        part = halves[half]
        sent["up", half].wait_recv()
        push(("upup", half), blocks.at[below], below, first, dev_up)
        sent["down", half].wait_recv()
        push(("downdown", half), blocks.at[above], above, second, dev_down)
        sent["x", half].wait_recv()
        push(("xup", half), blocks.at[other], other, part, dev_up)
        push(("xdown", half), blocks.at[other], other, part, dev_down)

    def pass_far(half):
        first, second = quarters[half]
        sent["upup", half].wait_recv()
        push(("far0", half), blocks.at[far], far, first, partner)
        sent["downdown", half].wait_recv()
        push(("far1", half), blocks.at[far], far, second, partner)

    def use(src, where, half, fresh=False):
        part = halves[half]
        value = src[part, :].astype(jnp.float32)
        square = value * value
        partial = (square[:, 0:128] + square[:, 128:256]) + (square[:, 256:384] + square[:, 384:512])
        cols = pl.ds(pl.multiple_of(where * width, width), width)
        scaled = (value * gain_ref[:, cols]).astype(jnp.bfloat16)
        term = jnp.dot(scaled, w_ref[cols, :], preferred_element_type=jnp.float32)
        squares[part, :] = partial if fresh else squares[part, :] + partial
        wide_acc[part, :] = term if fresh else wide_acc[part, :] + term

    def last_uses(half):
        for names, y in ((("xdown",), up), (("xup",), down), (("far0", "far1"), opposite)):
            for name in names:
                sent[name, half].wait_recv()
            use(blocks.at[slot(1 - x_lo, y)], slot(1 - x_lo, y), half)

    scale = head ** -0.5 * 1.4426950408889634

    def heads_out(half):
        part = halves[half]
        inverse = lax.rsqrt(jnp.sum(squares[part, :], axis=1, keepdims=True) / (N_CH * width) + norm_eps)
        for number in range(heads):
            for kind in range(3):
                first = (number * 3 + kind) * head
                value = wide_acc[part, first : first + head] * inverse
                if kind < 2:
                    value = value * cos_ref[part, :] + pltpu.roll(value, head // 2, 1) * sin_ref[part, :]
                if kind == 0:
                    value = value * scale
                qkv[number, kind, part, :] = value.astype(jnp.bfloat16)

    z_copies, q_copies, own_copies = {}, {}, []

    def exchange(half):
        part = halves[half]
        own_kv = pltpu.make_async_copy(qkv.at[z_pos, pl.ds(1, 2), part],
                                       keyvals.at[high, z_pos, :, core, part], own_sem.at[half, 1])
        own_q = pltpu.make_async_copy(qkv.at[z_pos, 0, part], queries.at[z_pos, part], own_sem.at[half, 0])
        own_kv.start()
        own_q.start()
        own_copies.append((own_kv, own_q))
        for step in (1, 2, 3):
            copy = remote(qkv.at[others[step - 1], pl.ds(1, 2), part], keyvals.at[high, z_pos, :, core, part],
                          z_send.at[half, step - 1], z_recv.at[half, step - 1], ring[step - 1])
            copy.start()
            z_copies[half, step] = copy
        for step in (1, 2, 3):
            copy = remote(qkv.at[others[step - 1], 0, part], queries.at[z_pos, part],
                          q_send.at[half, step - 1], q_recv.at[half, step - 1], ring[step - 1])
            copy.start()
            q_copies[half, step] = copy

    own_sends(0)
    loads[0].wait()
    use(stream_ref, mine, 0, True)
    pass_on(0)
    own_sends(1)
    use(blocks.at[above], above, 0)
    use(blocks.at[below], below, 0)
    use(blocks.at[other], other, 0)
    pass_far(0)
    use(blocks.at[far], far, 0)
    use(stream_ref, mine, 1, True)
    last_uses(0)
    heads_out(0)
    exchange(0)
    pass_on(1)
    use(blocks.at[above], above, 1)
    use(blocks.at[below], below, 1)
    pass_far(1)
    use(blocks.at[other], other, 1)
    use(blocks.at[far], far, 1)
    last_uses(1)
    heads_out(1)
    exchange(1)

    def source(step):
        return lax.rem(z_pos + N_Z - step, N_Z)

    shares, hops = [], []

    def spread(step, half):
        index = len(shares)
        place_here = keyvals.at[high, source(step), :, core, halves[half]]
        share = remote(place_here, place_here, s_send.at[index], s_recv.at[index], sibling)
        share.start()
        shares.append(share)
        if half == 0:
            hop = remote(place_here, place_here, h_send.at[index], h_recv.at[index], across)
        else:
            hop = remote(place_here, transit.at[step], h_send.at[index], h_recv.at[index], diagonal)
        hops.append(hop)

        @pl.when(high == 0)
        def _():
            hop.start()

    order = [(step, half) for half in range(2) for step in (0, 1, 3, 2)]
    for step, half in order:
        if step:
            z_copies[half, step].wait_recv()
        else:
            own_copies[half][0].wait()
        spread(step, half)
    for pair in own_copies:
        pair[1].wait()
    for copy in list(q_copies.values()) + shares:
        copy.wait_recv()

    span = 2 * rows
    row = lax.broadcasted_iota(jnp.int32, (tile, span), 0) + core * rows
    col = lax.broadcasted_iota(jnp.int32, (tile, span), 1)
    ones = jnp.ones((span, head), jnp.bfloat16)

    def piece_at(piece):
        return pl.ds(pl.multiple_of(piece * tile, tile), tile)

    def update(block, part, first, z, diagonal):
        fold(block, part, first, keyvals[high, z, 0].reshape(span, head), keyvals[high, z, 1].reshape(span, head), diagonal)

    def fold(block, part, first, keys, plain_values, diagonal):
        values = jnp.concatenate([plain_values, ones], axis=1)
        scores = lax.dot_general(queries[block, part], keys, (((1,), (1,)), ((), ())),
                                 preferred_element_type=jnp.float32)
        if diagonal:
            scores = jnp.where(col <= row + first, scores, -1e30)
        top = jnp.max(scores, axis=1, keepdims=True)
        if diagonal:
            new = jnp.broadcast_to(top, (tile, head))
        else:
            old = peak[block, part]
            new = jnp.maximum(old, top)
            shrink = jnp.exp2(old - new)
        peak[block, part] = new
        weights = jnp.exp2(scores - jnp.concatenate([new] * (span // head), axis=1)).astype(jnp.bfloat16)
        term = jnp.dot(weights, values, preferred_element_type=jnp.float32)
        if not diagonal:
            term = acc[block, part] * jnp.concatenate([shrink, shrink], axis=1) + term
        acc[block, part] = term

    def own_tile(piece):
        part, first = piece_at(piece), piece * tile
        for block in range(N_Z):
            update(block, part, first, block, True)
        for z in range(N_Z - 1):
            for block in range(z + 1, N_Z):
                update(block, part, first, z, False)

    def low_tile(piece, half):
        part, first = piece_at(piece), piece * tile

        def each(pair, carry):
            keys, values = [
                jnp.concatenate([keyvals[0, 2 * pair + number, kind, side, halves[half], :]
                                 for number in range(2) for side in range(2)], axis=0)
                for kind in range(2)
            ]
            for block in range(N_Z):
                fold(block, part, first, keys, values, False)
            return carry

        lax.fori_loop(0, N_Z // 2, each, 0)

    lanes = pl.ds(pl.multiple_of(z_pos * head, head), head)

    def result_copy(piece, block, owner):
        columns = pl.ds(pl.multiple_of(owner * head, head), head)
        part = piece_at(piece)
        return remote(results.at[block, part], attended.at[part, columns], o_send.at[piece, block],
                      o_recv.at[piece, owner], place(high, block, core))

    def partner_copy(piece, block, owner):
        columns = pl.ds(pl.multiple_of(owner * head, head), head)
        part = piece_at(piece)
        return remote(results.at[block, part], attended_in.at[part, columns], p_send.at[piece, block],
                      p_recv.at[piece, owner], partner_place(block))

    def complete(piece):
        part = piece_at(piece)

        def each(block, carry):
            total = acc[block, part]
            results[block, part] = (total[:, :head] / total[:, head:]).astype(jnp.bfloat16)
            partner_copy(piece, block, z_pos).start()

            @pl.when(block != z_pos)
            def _():
                result_copy(piece, block, z_pos).start()

            @pl.when(block == z_pos)
            def _():
                attended[part, lanes] = results[block, part]

            return carry

        lax.fori_loop(0, N_Z, each, 0)

    def way_place(way):
        return (ctx, x_lo * N_Y + lax.rem(y_pos + 1 + 2 * way, N_Y))

    def relay_copy(piece):
        steps = 1 + 2 * lax.rem(piece, 2) - piece // (PIECES - 1)
        return remote(relay_out.at[piece], relay_in.at[piece], r_send.at[piece], r_recv.at[piece],
                      (ctx, x_lo * N_Y + lax.rem(y_pos + steps, N_Y)))

    def direct_copy(way, piece):
        return remote(outbox.at[way, piece], inbox.at[way, piece], y_send.at[way, piece], y_recv.at[way, piece],
                      way_place(way))

    def multiply(piece):
        for z in others:
            result_copy(piece, z, z).wait_recv()
        for z in others + [z_pos]:
            partner_copy(piece, z, z).wait_recv()
        part = piece_at(piece)
        mine, theirs = attended[part, :], attended_in[part, :]

        def term(step):
            cols = pl.ds(pl.multiple_of(lax.rem(y_pos + step, N_Y) * width, width), width)
            return (jnp.dot(mine, w_own[:, cols], preferred_element_type=jnp.float32)
                    + jnp.dot(theirs, w_other[:, cols], preferred_element_type=jnp.float32))

        way = lax.rem(piece, 2)
        relay_out[piece] = term(2).astype(jnp.bfloat16)
        relay_copy(piece).start()
        outbox[1 - way, piece] = term(3 - 2 * way).astype(jnp.bfloat16)
        direct_copy(1 - way, piece).start()

        @pl.when(piece < PIECES - 1)
        def _():
            pending[piece] = term(1 + 2 * way)

        @pl.when(piece == PIECES - 1)
        def _():
            outbox[way, piece] = term(1 + 2 * way).astype(jnp.bfloat16)
            direct_copy(way, piece).start()

        kept[part, :] = term(0) + stream_ref[part, :].astype(jnp.float32)

    def combine(piece):
        relay_copy(piece).wait_recv()
        way = lax.rem(piece, 2)
        outbox[way, piece] = (pending[piece] + relay_in[piece].astype(jnp.float32)).astype(jnp.bfloat16)
        direct_copy(way, piece).start()

    @pl.when(high == 1)
    def _():
        passes, legs = [], []

        def landed(index):
            step, half = order[index]
            return keyvals.at[0, source(step), :, core, halves[half]]

        def forward(index):
            copy = remote(landed(index), landed(index), t_send.at[index], t_recv.at[index], sibling)
            copy.start()
            passes.append(copy)

        for index in range(4):
            hops[index].wait_recv()
            forward(index)
        for index in range(4, 8):
            own_tile(index - 4)
            hops[index].wait_recv()
            leg = remote(transit.at[order[index][0]], landed(index), d_send.at[index - 4], d_recv.at[index - 4], partner)
            leg.start()
            legs.append(leg)
        for copy in passes:
            copy.wait_recv()

        def each(piece, carry):
            low_tile(piece, 0)
            return carry

        lax.fori_loop(0, PIECES // 2, each, 0)
        for index in range(4, 8):
            legs[index - 4].wait_recv()
            forward(index)
        lax.fori_loop(PIECES // 2, PIECES, each, 0)
        for copy in passes[4:]:
            copy.wait_recv()
        for copy in passes:
            copy.wait_send()
        for leg in legs:
            leg.wait_send()

    loads[1].wait()
    loads[2].wait()

    def stage(step, carry):
        @pl.when(step < PIECES)
        def _():
            @pl.when(high == 0)
            def _():
                own_tile(step)

            @pl.when(high == 1)
            def _():
                low_tile(step, 1)

            complete(step)

        @pl.when(jnp.logical_and(step >= 1, step <= PIECES))
        def _():
            multiply(step - 1)

        @pl.when(jnp.logical_and(step >= 2, step <= PIECES))
        def _():
            combine(step - 2)

        return carry

    lax.fori_loop(0, PIECES + 1, stage, 0)

    def finish(piece, carry):
        part = piece_at(piece)
        direct_copy(0, piece).wait_recv()
        direct_copy(1, piece).wait_recv()

        @pl.when(piece == PIECES - 1)
        def _():
            relay_copy(piece).wait_recv()
            kept[part, :] = kept[part, :] + relay_in[piece].astype(jnp.float32)

        total = kept[part, :] + inbox[0, piece].astype(jnp.float32) + inbox[1, piece].astype(jnp.float32)
        out_ref[part, :] = total.astype(jnp.bfloat16)
        return carry

    lax.fori_loop(0, PIECES, finish, 0)

    def drain(piece, carry):
        for z in others:
            result_copy(piece, z, z_pos).wait_send()
        for z in others + [z_pos]:
            partner_copy(piece, z, z_pos).wait_send()
        relay_copy(piece).wait_send()
        direct_copy(0, piece).wait_send()
        direct_copy(1, piece).wait_send()
        return carry

    lax.fori_loop(0, PIECES, drain, 0)
    for copy in list(sent.values()) + list(z_copies.values()) + list(q_copies.values()) + shares:
        copy.wait_send()

    @pl.when(high == 0)
    def _():
        for hop in hops:
            hop.wait_send()


def attention(stream, gain_row, cosine, sine, weight, own_weight, other_half):
    rows, width = stream.shape
    head = HEAD
    dma = pltpu.SemaphoreType.DMA
    return pl.pallas_call(
        attention_kernel,
        out_shape=jax.ShapeDtypeStruct((rows, width), jnp.bfloat16),
        in_specs=whole(4) + [pl.BlockSpec(memory_space=pl.ANY)] * 3,
        out_specs=pl.BlockSpec(memory_space=pltpu.VMEM),
        scratch_shapes=[
            pltpu.VMEM((N_CH, rows, width), jnp.bfloat16),
            pltpu.VMEM(weight.shape, jnp.bfloat16),
            pltpu.VMEM((rows, weight.shape[1]), jnp.float32),
            pltpu.VMEM((rows, 128), jnp.float32),
            pltpu.VMEM((width // head, 3, rows, head), jnp.bfloat16),
            pltpu.VMEM((N_Z, rows, head), jnp.bfloat16),
            pltpu.VMEM((2, N_Z, 2, 2, rows, head), jnp.bfloat16),
            pltpu.VMEM((N_Z, rows, 2 * head), jnp.float32),
            pltpu.VMEM((N_Z, rows, head), jnp.float32),
            pltpu.VMEM((N_Z, rows, head), jnp.bfloat16),
            pltpu.VMEM((rows, width), jnp.bfloat16),
            pltpu.VMEM((rows, width), jnp.bfloat16),
            pltpu.VMEM((width, N_Y * width), jnp.bfloat16),
            pltpu.VMEM((width, N_Y * width), jnp.bfloat16),
        ] + box_shapes(rows, width) + [
            dma((3,)), dma((18,)), dma((18,)), dma((2, 2)), dma((2, 3)), dma((2, 3)), dma((2, 3)), dma((2, 3)),
            dma((8,)), dma((8,)), dma((8,)), dma((8,)), dma((8,)), dma((8,)),
            dma((PIECES, N_Z)), dma((PIECES, N_Z)), dma((PIECES, N_Z)), dma((PIECES, N_Z)),
            pltpu.VMEM((N_Z, 2, rows // 2, head), jnp.bfloat16), dma((4,)), dma((4,)),
        ],
        compiler_params=pltpu.CompilerParams(collective_id=3, has_side_effects=True, vmem_limit_bytes=VMEM_LIMIT),
        name="attention",
    )(stream, gain_row, cosine, sine, weight, own_weight, other_half)


def rotation_tables(rows):
    positions = lax.axis_index("ctx") * rows + jnp.arange(rows, dtype=jnp.int32)
    half_size = HEAD // 2
    frequency = 10000.0 ** (-jnp.arange(half_size, dtype=jnp.float32) * 2.0 / HEAD)
    angles = positions.astype(jnp.float32)[:, None] * frequency[None, :]
    cosine, sine = jnp.cos(angles), jnp.sin(angles)
    return jnp.concatenate([cosine, cosine], axis=1), jnp.concatenate([-sine, sine], axis=1)


def shards(features, residual_in, short_filter, medium_filter, skip_gain, out_weight, norm_gain, attn_weight,
           attn_out):
    rows = features.shape[0]
    cosine, sine = rotation_tables(rows)
    stream, attn_half = hyena(jnp.transpose(features, (1, 0, 2)), short_filter, medium_filter.T,
                              skip_gain[None, :], residual_in, out_weight, attn_out)
    return attention(stream, norm_gain[None, :], cosine, sine, attn_weight, attn_out, attn_half)


def solution(mesh):
    in_specs = (
        P("ctx", None, "ch"),
        P("ctx", "ch"),
        P(None, None, "ch"),
        P(None, "ch"),
        P("ch"),
        P("ch", None),
        P(),
        P(None, "ch"),
        P("ch", None),
    )
    out_specs = P("ctx", "ch")
    return jax.shard_map(shards, mesh=mesh, in_specs=in_specs, out_specs=out_specs, check_vma=False)
```
